256 devices in a mesh: row: 16 (over y, x_hi, core), col: 16 (over z, x_lo).
Axes of the slice: x: 4 (x_hi: 2, x_lo: 2; x = x_hi * 2 + x_lo), y: 4, z: 8, core: 2. Of those that a mesh axis runs over, the one named last changes fastest.
Arguments:
- pair_rep: bfloat16 [1024, 1024, 128], P('row', 'col'), may hold values from -6 to 6
- token_mask: int32 [1024], replicated, may hold values from 0 to 1, as said below
- in_gain: float32 [128], replicated, may hold values from 0.5 to 2
- in_bias: float32 [128], replicated, may hold values from -3 to 3
- left_weight: bfloat16 [128, 256], replicated, may hold values from -0.5 to 0.5
- right_weight: bfloat16 [128, 256], replicated, may hold values from -0.5 to 0.5
- gate_weight: bfloat16 [128, 128], replicated, may hold values from -0.5 to 0.5
- out_gain: float32 [128], replicated, may hold values from 0.5 to 2
- out_bias: float32 [128], replicated, may hold values from -3 to 3
- out_weight: bfloat16 [128, 128], replicated, may hold values from -0.5 to 0.5
Outputs:
- update: bfloat16 [1024, 1024, 128], P('row', 'col')
The draws below stay inside these ranges and needn't reach their ends.
Inputs may be any that keep to these rules, and one draw needn't show every extreme that they name: `token_mask`: tokens lie in chains of 64 consecutive slots; in each chain a leading run of 32 to 64 slots is 1 and the rest is 0; the first chain is full and the second holds exactly 32 real tokens.
All inputs are finite; a program needn't handle non-finite values.
Results may differ from the reference program's by a relative error of at most 0.0053.
Values may be sent and summed in bfloat16 or wider, within the bound.
A program may use at most 128 MiB of HBM per device.

```python
import math
import jax
import jax.numpy as jnp
from jax import lax

PAIR = 128
HID = 128
CHAIN = 64
TOKENS = 1024


def draw_token_mask(key, part):
    chains = TOKENS // CHAIN
    lengths = jax.random.randint(key, (chains,), CHAIN // 2, CHAIN + 1).astype(jnp.int32)
    lengths = lengths.at[0].set(CHAIN).at[1].set(CHAIN // 2)
    slots = jnp.arange(TOKENS, dtype=jnp.int32)
    owner = slots // CHAIN
    return (slots % CHAIN < lengths[owner]).astype(jnp.int32)


def levels(stream_key, shape, pieces, low, top_value):
    def one(dim, blocks):
        heights = jax.random.uniform(jax.random.fold_in(jax.random.fold_in(stream_key, 6), dim), (blocks,), jnp.float32, low / len(pieces), top_value / len(pieces))
        return jnp.repeat(jnp.exp(heights), shape[dim] // blocks).reshape((-1,) + (1,) * (len(shape) - dim - 1))

    gain = one(*pieces[0])
    for cut in pieces[1:]:
        gain = gain * one(*cut)
    return gain


def scatter_about(key, dims, scale, limit, cuts=(), kind=jnp.bfloat16):
    values = scale * jax.random.normal(key, dims, jnp.float32)
    if cuts:
        values = values * levels(key, dims, cuts, -0.22, 0.18)
    return jnp.clip(values, -limit, limit).astype(kind)


def setup_inputs(seed: int = 0) -> dict:
    key_list = jax.random.split(jax.random.key(seed), 11)
    pair_rep = scatter_about(key_list[0], (TOKENS, TOKENS, PAIR), 1.0, 6.0, ((0, 16), (1, 16)))
    token_mask = draw_token_mask(jax.random.fold_in(key_list[10], 71), 0)
    in_gain = jnp.clip(jnp.exp(jax.random.uniform(key_list[2], (PAIR,), jnp.float32, math.log(0.5), math.log(2.0))), 0.5, 2.0)
    in_bias = scatter_about(key_list[3], (PAIR,), 0.5, 3.0, (), jnp.float32)
    left_weight = scatter_about(key_list[4], (PAIR, 2 * HID), PAIR ** -0.5, 0.5)
    right_weight = scatter_about(key_list[5], (PAIR, 2 * HID), PAIR ** -0.5, 0.5)
    gate_weight = scatter_about(key_list[6], (PAIR, PAIR), PAIR ** -0.5, 0.5)
    out_gain = jnp.clip(jnp.exp(jax.random.uniform(key_list[7], (HID,), jnp.float32, math.log(0.5), math.log(2.0))), 0.5, 2.0)
    out_bias = scatter_about(key_list[8], (HID,), 0.5, 3.0, (), jnp.float32)
    out_weight = scatter_about(key_list[9], (HID, PAIR), HID ** -0.5, 0.5)
    return dict(pair_rep=pair_rep, token_mask=token_mask, in_gain=in_gain, in_bias=in_bias, left_weight=left_weight, right_weight=right_weight, gate_weight=gate_weight, out_gain=out_gain, out_bias=out_bias, out_weight=out_weight)


EPS = 1e-05

def layer_norm(values, gain_vec, bias_vec):
    average = lax.optimization_barrier(jnp.mean(values, axis=-1, keepdims=True))
    centered = values - average
    variance = lax.optimization_barrier(jnp.mean(centered * centered, axis=-1, keepdims=True))
    return centered * lax.rsqrt(variance + EPS) * gain_vec + bias_vec

def edge_values(normed, weight, pair_mask):
    projected = jnp.dot(normed, weight, preferred_element_type=jnp.float32)
    return (jax.nn.sigmoid(projected[:, :HID]) * projected[:, HID:] * pair_mask).astype(jnp.bfloat16)

def reference(pair_rep, token_mask, in_gain, in_bias, left_weight, right_weight, gate_weight, out_gain, out_bias, out_weight):
    flat_pair = pair_rep.reshape(TOKENS * TOKENS, PAIR).astype(jnp.float32)
    normed = layer_norm(flat_pair, in_gain, in_bias).astype(jnp.bfloat16)
    validity = token_mask.astype(jnp.float32)
    pair_mask = (validity[:, None] * validity[None, :]).reshape(TOKENS * TOKENS, 1)
    left_value = edge_values(normed, left_weight, pair_mask)
    right_value = edge_values(normed, right_weight, pair_mask)
    gate_value = jax.nn.sigmoid(jnp.dot(normed, gate_weight, preferred_element_type=jnp.float32))
    left_first = left_value.reshape(TOKENS, TOKENS, HID).transpose(2, 0, 1).astype(jnp.float32)
    right_first = right_value.reshape(TOKENS, TOKENS, HID).transpose(2, 0, 1).astype(jnp.float32)
    product = jnp.einsum('hik,hjk->hij', left_first, right_first, precision=lax.Precision.HIGHEST)
    product = product.transpose(1, 2, 0).reshape(TOKENS * TOKENS, HID)
    final_norm = layer_norm(product, out_gain, out_bias).astype(jnp.bfloat16)
    update = gate_value * jnp.dot(final_norm, out_weight, preferred_element_type=jnp.float32)
    return update.reshape(TOKENS, TOKENS, PAIR).astype(jnp.bfloat16)
```

```python
import functools

import jax
import jax.numpy as jnp
from jax import lax
from jax.experimental import pallas as pl
from jax.experimental.pallas import tpu as pltpu
from jax.sharding import PartitionSpec as P

EPS = 1e-05
MESH = pl.DeviceIdType.MESH
F32 = jnp.float32
BF16 = jnp.bfloat16
NT = (((1,), (1,)), ((), ()))
TN = (((0,), (0,)), ((), ()))

ROWS = 16
COLS = 16
CHIPS = 8
DEPTHS = 8
TOK = 64
WIDTH = 128
HALF = 8


def sigmoid(v):
    return 0.5 * jnp.tanh(0.5 * v) + 0.5


def shift_of(step):
    away = (step + 1) // 2
    return lax.rem(4 + (1 - 2 * lax.rem(step, 2)) * away, DEPTHS)


def exchange_kernel(
    x_ref, w_ref, wg_ref, ln_ref, m_ref,
    q_ref, gate_ref,
    t_buf, s_buf, x_buf, acc, p_buf, gate_buf,
    gate_sem, s_send, s_recv, f_send, f_recv, p_send, p_recv,
):
    row, col = lax.axis_index("row"), lax.axis_index("col")
    core, half, chip, slot = lax.rem(row, 2), row // HALF, row // 2, lax.rem(row, HALF)
    depth, side = col // 2, lax.rem(col, 2)
    me = row * COLS + col
    sibling = row + 1 - 2 * core
    channel = chip * COLS + col

    barrier = pltpu.get_barrier_semaphore()

    def greet(t, carry):
        other = lax.rem(me + t, ROWS * COLS)
        pl.semaphore_signal(
            barrier, inc=1, device_id=(other // COLS, lax.rem(other, COLS)), device_id_type=MESH
        )
        return carry

    lax.fori_loop(1, ROWS * COLS, greet, 0)

    gain, bias = ln_ref[0:1, :], ln_ref[1:2, :]
    blank = jnp.zeros((TOK, WIDTH), BF16)

    def project(q, carry):
        v = x_ref[pl.ds(2 * q, 2)].reshape(2 * TOK, WIDTH).astype(F32)
        v = v - jnp.mean(v, axis=-1, keepdims=True)
        spread = jnp.mean(v * v, axis=-1, keepdims=True)
        n = (v * lax.rsqrt(spread + EPS) * gain + bias).astype(BF16)
        gate = sigmoid(jnp.dot(n, wg_ref[...], preferred_element_type=F32))
        gate_buf[pl.ds(2 * q, 2)] = gate.reshape(2, TOK, WIDTH)
        a, b = n[:TOK], n[TOK:]
        both = jnp.concatenate(
            [jnp.concatenate([a, blank, b, blank], 0), jnp.concatenate([blank, a, blank, b], 0)], 1
        )
        d = lax.dot_general(w_ref[...], both, NT, preferred_element_type=F32)
        e = sigmoid(d[:WIDTH]) * d[WIDTH:]
        base = pl.multiple_of(q * 2 * WIDTH, 2 * WIDTH)
        t_buf[pl.ds(base, WIDTH), :] = e[:, :WIDTH] * m_ref[pl.ds(2 * q, 1), :]
        t_buf[pl.ds(base + WIDTH, WIDTH), :] = e[:, WIDTH:] * m_ref[pl.ds(2 * q + 1, 1), :]
        return carry

    lax.fori_loop(0, TOK // 2, project, 0)
    gate_copy = pltpu.make_async_copy(gate_buf, gate_ref, gate_sem)
    gate_copy.start()

    def by_channel(h, carry):
        s_buf[h] = t_buf[pl.ds(h, TOK, stride=WIDTH), :].astype(BF16)
        return carry

    lax.fori_loop(0, WIDTH, by_channel, 0)

    pl.semaphore_wait(barrier, ROWS * COLS - 1)

    def send(step, t):
        to_chip = lax.rem(chip + t // 2, CHIPS)
        to_col = lax.rem(depth + shift_of(step), DEPTHS) * 2 + lax.rem(side + t, 2)
        to_row = to_chip * 2 + half
        src, dst = s_buf.at[to_chip * COLS + to_col], x_buf.at[col, row]
        mine = jnp.logical_and(to_row == row, to_col == col)

        @pl.when(mine)
        def _():
            pltpu.make_async_copy(src, dst, s_recv.at[step]).start()

        @pl.when(jnp.logical_not(mine))
        def _():
            pltpu.make_async_remote_copy(
                src_ref=src, dst_ref=dst, send_sem=s_send, recv_sem=s_recv.at[step],
                device_id=(to_row, to_col), device_id_type=MESH,
            ).start()

    def send_one(step, t, carry):
        send(step, t)
        return carry

    def send_two(u, carry):
        step = 1 + 2 * (u // 16)
        send(step, lax.rem(u, 16))
        send(step + 1, lax.rem(u, 16))
        return carry

    lax.fori_loop(0, 16, functools.partial(send_one, 0), 0)
    lax.fori_loop(0, 48, send_two, 0)
    lax.fori_loop(0, 16, functools.partial(send_one, 7), 0)

    lanes = lax.broadcasted_iota(jnp.int32, (HALF * TOK, WIDTH), 1)

    def first_col(step):
        return lax.rem(depth - shift_of(step) + DEPTHS, DEPTHS) * 2

    def forward(step):
        part = x_buf.at[pl.ds(first_col(step), 2), pl.ds(core * HALF, HALF)]
        return pltpu.make_async_remote_copy(
            src_ref=part, dst_ref=part, send_sem=f_send.at[step], recv_sem=f_recv.at[step],
            device_id=(sibling, col), device_id_type=MESH,
        )

    def arrive(step):
        part = x_buf.at[pl.ds(first_col(step), 2), pl.ds(core * HALF, HALF)]
        pltpu.make_async_copy(part, part, s_recv.at[step]).wait()
        forward(step).start()

    def multiply(step, first):
        forward(step).wait_recv()
        c = first_col(step)
        wide = []
        for e in range(2):
            own = x_buf[c + e, pl.ds(core * HALF, HALF)].reshape(HALF * TOK, WIDTH).astype(F32)
            wide.append(jnp.where(lanes >= TOK, pltpu.roll(own, TOK, 1), 0.0).astype(BF16))
        own = jnp.concatenate(wide, 1)

        def block(n, carry):
            others = jnp.concatenate(
                [x_buf[c + e, pl.ds(4 * n, 4)].reshape(4 * TOK, WIDTH) for e in range(2)], 1
            )
            part = lax.dot_general(own, others, NT, preferred_element_type=F32)
            acc[n] = part if first else acc[n] + part
            return carry

        lax.fori_loop(0, 4, block, 0)

    arrive(0)
    arrive(1)
    multiply(0, True)

    def middle(step, carry):
        arrive(step + 1)
        multiply(step, False)
        return carry

    lax.fori_loop(1, DEPTHS - 1, middle, 0)
    multiply(DEPTHS - 1, False)

    low = lanes[: TOK // 2] < TOK

    def give(u, carry):
        r = lax.rem(slot + u, HALF)
        for n in range(4):
            for m in range(2):
                v = acc[n, pl.ds(pl.multiple_of(r * TOK, TOK), TOK), m * WIDTH : (m + 1) * WIDTH]
                top, bot = v[: TOK // 2], v[TOK // 2 :]
                even = jnp.where(low, top, pltpu.roll(bot, TOK, 1))
                odd = jnp.where(low, pltpu.roll(top, TOK, 1), bot)
                p_buf[r, 4 * n + 2 * m] = even.astype(BF16)
                p_buf[r, 4 * n + 2 * m + 1] = odd.astype(BF16)

        to_row = core * HALF + r

        def give_one(t, carry):
            step = t // 2
            to_col = lax.rem(depth + shift_of(step), DEPTHS) * 2 + lax.rem(side + t, 2)
            src, dst = p_buf.at[r, to_col], q_ref.at[channel]
            mine = jnp.logical_and(to_row == row, to_col == col)

            @pl.when(mine)
            def _():
                pltpu.make_async_copy(src, dst, p_recv).start()

            @pl.when(jnp.logical_not(mine))
            def _():
                pltpu.make_async_remote_copy(
                    src_ref=src, dst_ref=dst, send_sem=p_send, recv_sem=p_recv,
                    device_id=(to_row, to_col), device_id_type=MESH,
                ).start()

            return carry

        lax.fori_loop(0, COLS, give_one, 0)
        return carry

    lax.fori_loop(0, HALF, give, 0)

    gate_copy.wait()
    pltpu.make_async_copy(q_ref, q_ref, p_recv).wait()

    def drain(step, carry):
        forward(step).wait_send()
        return carry

    lax.fori_loop(0, DEPTHS, drain, 0)
    count = WIDTH - 1
    itself = half == core

    @pl.when(itself)
    def _():
        sent = s_buf.at[pl.ds(0, count)]
        pltpu.make_async_copy(sent, sent, s_send).wait()
        given = q_ref.at[pl.ds(0, count)]
        pltpu.make_async_copy(given, given, p_send).wait()

    @pl.when(jnp.logical_not(itself))
    def _():
        pltpu.make_async_copy(s_buf, s_buf, s_send).wait()
        pltpu.make_async_copy(q_ref, q_ref, p_send).wait()


def exchange(pair, w, wg, ln, mask):
    whole = pl.BlockSpec(memory_space=pltpu.VMEM)
    return pl.pallas_call(
        exchange_kernel,
        out_shape=(
            jax.ShapeDtypeStruct((WIDTH, TOK // 2, WIDTH), BF16),
            jax.ShapeDtypeStruct((TOK, TOK, WIDTH), F32),
        ),
        in_specs=[whole] * 5,
        out_specs=(pl.BlockSpec(memory_space=pl.ANY), pl.BlockSpec(memory_space=pl.ANY)),
        scratch_shapes=[
            pltpu.VMEM((TOK * WIDTH, WIDTH), F32),
            pltpu.VMEM((WIDTH, TOK, WIDTH), BF16),
            pltpu.VMEM((COLS, ROWS, TOK, WIDTH), BF16),
            pltpu.VMEM((4, HALF * TOK, 4 * TOK), F32),
            pltpu.VMEM((HALF, COLS, TOK // 2, WIDTH), BF16),
            pltpu.VMEM((TOK, TOK, WIDTH), F32),
            pltpu.SemaphoreType.DMA,
            pltpu.SemaphoreType.DMA,
            pltpu.SemaphoreType.DMA((DEPTHS,)),
            pltpu.SemaphoreType.DMA((DEPTHS,)),
            pltpu.SemaphoreType.DMA((DEPTHS,)),
            pltpu.SemaphoreType.DMA,
            pltpu.SemaphoreType.DMA,
        ],
        compiler_params=pltpu.CompilerParams(collective_id=0, has_side_effects=True),
        name="exchange",
    )(pair, w, wg, ln, mask)


CHUNK = 8


def update_kernel(q_ref, gate_ref, g_ref, b_ref, w_ref, out_ref, buf):
    v = q_ref[...].astype(F32)
    v = v - jnp.mean(v, axis=0, keepdims=True)
    spread = jnp.mean(v * v, axis=0, keepdims=True)
    n = v * lax.rsqrt(spread + EPS) * g_ref[...] + b_ref[...]
    buf[...] = n.reshape(WIDTH * CHUNK, WIDTH)
    for q in range(CHUNK):
        n = buf[pl.ds(q, WIDTH, stride=CHUNK), :].astype(BF16)
        o = lax.dot_general(n, w_ref[...], TN, preferred_element_type=F32)
        out_ref[0, q] = (gate_ref[0, q] * o[:TOK]).astype(BF16)
        out_ref[1, q] = (gate_ref[1, q] * o[TOK:]).astype(BF16)


def finish(q, gate, gain, bias, w):
    whole = lambda shape: pl.BlockSpec(shape, lambda i: (0,) * len(shape))
    part = pl.BlockSpec((2, CHUNK, TOK, WIDTH), lambda i: (0, i, 0, 0))
    return pl.pallas_call(
        update_kernel,
        out_shape=jax.ShapeDtypeStruct((2, TOK // 2, TOK, WIDTH), BF16),
        grid=(TOK // 2 // CHUNK,),
        in_specs=[
            pl.BlockSpec((WIDTH, CHUNK, WIDTH), lambda i: (0, i, 0)),
            part,
            whole((WIDTH, 1, WIDTH)),
            whole((WIDTH, 1, WIDTH)),
            whole((WIDTH, WIDTH)),
        ],
        out_specs=part,
        scratch_shapes=[pltpu.VMEM((WIDTH * CHUNK, WIDTH), F32)],
        name="finish",
    )(q, gate, gain, bias, w)


def shards(
    pair_rep,
    token_mask,
    in_gain,
    in_bias,
    left_weight,
    right_weight,
    gate_weight,
    out_gain,
    out_bias,
    out_weight,
):
    valid = token_mask.astype(F32)
    row_valid = lax.dynamic_slice_in_dim(valid, lax.axis_index("row") * TOK, TOK)
    col_valid = lax.dynamic_slice_in_dim(valid, lax.axis_index("col") * TOK, TOK)
    mask = row_valid[:, None] * jnp.tile(col_valid, 2)[None, :]
    w = jnp.concatenate([left_weight.T, right_weight.T], axis=1)
    ln = jnp.stack([in_gain, in_bias])
    q, gate = exchange(pair_rep, w, gate_weight, ln, mask)
    spread = lambda v: jnp.broadcast_to(v[:, None, None], (WIDTH, 1, WIDTH))
    out = finish(
        q, gate.reshape(2, TOK // 2, TOK, WIDTH), spread(out_gain), spread(out_bias), out_weight
    )
    return out.reshape(TOK, TOK, WIDTH)


def solution(mesh):
    placed = (P("row", "col", None), P(), P(), P(), P(), P(), P(), P(), P(), P())
    return jax.shard_map(
        shards, mesh=mesh, in_specs=placed, out_specs=P("row", "col", None), check_vma=False
    )
```

```python
import functools

import jax
import jax.numpy as jnp
from jax import lax
from jax.experimental import pallas as pl
from jax.experimental.pallas import tpu as pltpu
from jax.sharding import PartitionSpec as P

EPS = 1e-05
MESH = pl.DeviceIdType.MESH
F32 = jnp.float32
BF16 = jnp.bfloat16
NT = (((1,), (1,)), ((), ()))
TN = (((0,), (0,)), ((), ()))

ROWS = 16
COLS = 16
CHIPS = 8
DEPTHS = 8
TOK = 64
WIDTH = 128
HALF = 8


def sigmoid(v):
    return 0.5 * jnp.tanh(0.5 * v) + 0.5


SHIFTS = (4, 3, 5, 2, 6, 1, 7, 0)
PARTS = 4
PART = TOK // PARTS


def shift_of(step):
    away = (step + 1) // 2
    return lax.rem(4 + (1 - 2 * lax.rem(step, 2)) * away, DEPTHS)


def exchange_kernel(
    mask_ref, x_ref, wl_ref, wr_ref, wg_ref, gain_ref, bias_ref, valid_ref,
    q_ref, gate_ref,
    n_buf, t_buf, s_buf, x_buf, acc, p_buf, gate_buf,
    gate_sem, s_send, s_recv, f_send, f_recv, p_send, p_recv,
):
    row, col = lax.axis_index("row"), lax.axis_index("col")
    core, half, chip, slot = lax.rem(row, 2), row // HALF, row // 2, lax.rem(row, HALF)
    depth, side = col // 2, lax.rem(col, 2)
    sibling = row + 1 - 2 * core
    channel = chip * COLS + col
    itself = half == core
    apart = jnp.logical_not(itself)

    barrier = pltpu.get_barrier_semaphore()

    def hello(to_row, to_col):
        pl.semaphore_signal(barrier, inc=1, device_id=(to_row, to_col), device_id_type=MESH)

    def greet(c, carry):
        for r in range(HALF):
            to_row = core * HALF + r
            pl.when(jnp.logical_not(jnp.logical_and(to_row == row, c == col)))(
                functools.partial(hello, to_row, c)
            )
        return carry

    lax.fori_loop(0, COLS, greet, 0)
    pl.when(apart)(functools.partial(hello, sibling, col))

    gain, bias = gain_ref[...], bias_ref[...]
    wide = 2 * WIDTH
    eye = lax.broadcasted_iota(jnp.int32, (wide, wide), 0)
    eye = jnp.where(eye == lax.broadcasted_iota(jnp.int32, (wide, wide), 1), 1.0, 0.0).astype(BF16)
    weight = jnp.concatenate(
        [
            lax.dot_general(eye, w[...], NT, preferred_element_type=F32).astype(BF16)
            for w in (wl_ref, wr_ref)
        ],
        1,
    )
    blank = jnp.zeros((TOK, WIDTH), BF16)
    lane = lax.broadcasted_iota(jnp.int32, (1, WIDTH), 1)
    held = valid_ref[pl.ds(depth, 1), :].astype(F32)
    near = jnp.where(side == 0, 1, 0) == jnp.where(lane < TOK, 1, 0)
    held = jnp.where(near, held, pltpu.roll(held, TOK, 1))

    def project(part):
        for u in range(PART // 2):
            i = part * PART + 2 * u
            v = x_ref[pl.ds(i, 2)].reshape(2 * TOK, WIDTH).astype(F32)
            v = v - jnp.mean(v, axis=-1, keepdims=True)
            spread = jnp.mean(v * v, axis=-1, keepdims=True)
            n = (v * lax.rsqrt(spread + EPS) * gain + bias).astype(BF16)
            n_buf[pl.ds(i, 2)] = n.reshape(2, TOK, WIDTH)
            a, b = n[:TOK], n[TOK:]
            both = jnp.concatenate(
                [
                    jnp.concatenate([a, blank, b, blank], 0),
                    jnp.concatenate([blank, a, blank, b], 0),
                ],
                1,
            )
            d = lax.dot_general(weight, both, NT, preferred_element_type=F32)
            e = sigmoid(d[:WIDTH]) * d[WIDTH:]
            for k in range(2):
                m = held * mask_ref[row * TOK + i + k].astype(F32)
                t_buf[2 * u + k] = (e[:, k * WIDTH : (k + 1) * WIDTH] * m).astype(BF16)
        s_buf[:, pl.ds(part * PART, PART), :] = jnp.swapaxes(t_buf[...], 0, 1)

    chips = [lax.rem(chip + d, CHIPS) for d in range(CHIPS)]
    sides = [side, 1 - side]

    def send_to(part, step, d, to_col, alone):
        rows = pl.ds(part * PART, PART)
        src = s_buf.at[chips[d] * COLS + to_col, rows]
        dst = x_buf.at[col, row, rows]

        def remote():
            pltpu.make_async_remote_copy(
                src_ref=src, dst_ref=dst, send_sem=s_send, recv_sem=s_recv.at[step],
                device_id=(chips[d] * 2 + half, to_col), device_id_type=MESH,
            ).start()

        def local():
            pltpu.make_async_copy(src, dst, s_recv.at[step]).start()

        if alone:
            pl.when(itself)(local)
            pl.when(apart)(remote)
        else:
            remote()

    def send(part):
        far = lax.rem(depth + 4, DEPTHS) * 2
        for d in range(CHIPS):
            for e in range(2):
                send_to(part, 0, d, far + sides[e], False)

        def pair(u, carry):
            down = lax.rem(depth + 4 - u, DEPTHS) * 2
            up = lax.rem(depth + 4 + u, DEPTHS) * 2
            for d in range(CHIPS):
                for e in range(2):
                    send_to(part, 2 * u - 1, d, down + sides[e], False)
                    send_to(part, 2 * u, d, up + sides[e], False)
            return carry

        lax.fori_loop(1, 4, pair, 0)
        for d in range(CHIPS):
            for e in range(2):
                send_to(part, 7, d, depth * 2 + sides[e], d == 0 and e == 0)

    project(0)
    pl.semaphore_wait(barrier, CHIPS * COLS)
    send(0)

    def rest(part, carry):
        project(part)
        send(part)
        return carry

    lax.fori_loop(1, PARTS, rest, 0)

    def gates(u, carry):
        n = n_buf[pl.ds(4 * u, 4)].reshape(4 * TOK, WIDTH)
        gate = sigmoid(jnp.dot(n, wg_ref[...], preferred_element_type=F32))
        gate_buf[pl.ds(4 * u, 4)] = gate.reshape(4, TOK, WIDTH)
        return carry

    lax.fori_loop(0, TOK // 4, gates, 0)
    gate_copy = pltpu.make_async_copy(gate_buf, gate_ref, gate_sem)
    gate_copy.start()

    lanes = lax.broadcasted_iota(jnp.int32, (HALF * TOK, WIDTH), 1)

    def first_col(step):
        return lax.rem(depth - shift_of(step) + DEPTHS, DEPTHS) * 2

    def forward(step):
        part = x_buf.at[pl.ds(first_col(step), 2), pl.ds(core * HALF, HALF)]
        return pltpu.make_async_remote_copy(
            src_ref=part, dst_ref=part, send_sem=f_send.at[step], recv_sem=f_recv.at[step],
            device_id=(sibling, col), device_id_type=MESH,
        )

    def arrive(step):
        part = x_buf.at[pl.ds(first_col(step), 2), pl.ds(core * HALF, HALF)]
        pltpu.make_async_copy(part, part, s_recv.at[step]).wait()
        forward(step).start()

    def multiply(step, first):
        forward(step).wait_recv()
        c = first_col(step)
        own = []
        for e in range(2):
            v = x_buf[c + e, pl.ds(core * HALF, HALF)].reshape(HALF * TOK, WIDTH).astype(F32)
            own.append(jnp.where(lanes >= TOK, pltpu.roll(v, TOK, 1), 0.0).astype(BF16))
        own = jnp.concatenate(own, 1)

        def block(n, carry):
            others = jnp.concatenate(
                [x_buf[c + e, pl.ds(4 * n, 4)].reshape(4 * TOK, WIDTH) for e in range(2)], 1
            )
            part = lax.dot_general(own, others, NT, preferred_element_type=F32)
            acc[n] = part if first else acc[n] + part
            return carry

        lax.fori_loop(0, 4, block, 0)

    arrive(0)
    arrive(1)
    multiply(0, True)

    def middle(step, carry):
        arrive(step + 1)
        multiply(step, False)
        return carry

    lax.fori_loop(1, DEPTHS - 1, middle, 0)
    multiply(DEPTHS - 1, False)

    low = lanes[: TOK // 2] < TOK
    targets = [
        lax.rem(depth + shift, DEPTHS) * 2 + sides[e] for shift in SHIFTS for e in range(2)
    ]

    def give(u, carry):
        r = lax.rem(slot + u, HALF)
        for n in range(4):
            for m in range(2):
                v = acc[n, pl.ds(pl.multiple_of(r * TOK, TOK), TOK), m * WIDTH : (m + 1) * WIDTH]
                top, bot = v[: TOK // 2], v[TOK // 2 :]
                even = jnp.where(low, top, pltpu.roll(bot, TOK, 1))
                odd = jnp.where(low, pltpu.roll(top, TOK, 1), bot)
                p_buf[r, 4 * n + 2 * m] = even.astype(BF16)
                p_buf[r, 4 * n + 2 * m + 1] = odd.astype(BF16)
        to_row = core * HALF + r
        for k, to_col in enumerate(targets):
            src, dst = p_buf.at[r, to_col], q_ref.at[channel]

            def remote(src=src, dst=dst, to_col=to_col):
                pltpu.make_async_remote_copy(
                    src_ref=src, dst_ref=dst, send_sem=p_send, recv_sem=p_recv,
                    device_id=(to_row, to_col), device_id_type=MESH,
                ).start()

            def local(src=src, dst=dst):
                pltpu.make_async_copy(src, dst, p_recv).start()

            if SHIFTS[k // 2] == 0 and k % 2 == 0:
                here = to_row == row
                pl.when(here)(local)
                pl.when(jnp.logical_not(here))(remote)
            else:
                remote()
        return carry

    lax.fori_loop(0, HALF, give, 0)

    gate_copy.wait()
    pltpu.make_async_copy(q_ref, q_ref, p_recv).wait()

    def drain(step, carry):
        forward(step).wait_send()
        return carry

    lax.fori_loop(0, DEPTHS, drain, 0)

    @pl.when(itself)
    def _():
        sent = s_buf.at[pl.ds(0, WIDTH - 1)]
        pltpu.make_async_copy(sent, sent, s_send).wait()
        given = q_ref.at[pl.ds(0, WIDTH - 1)]
        pltpu.make_async_copy(given, given, p_send).wait()

    @pl.when(apart)
    def _():
        pltpu.make_async_copy(s_buf, s_buf, s_send).wait()
        pltpu.make_async_copy(q_ref, q_ref, p_send).wait()


def exchange(mask, pair, wl, wr, wg, gain, bias):
    whole = pl.BlockSpec(memory_space=pltpu.VMEM)
    return pl.pallas_call(
        exchange_kernel,
        out_shape=(
            jax.ShapeDtypeStruct((WIDTH, TOK // 2, WIDTH), BF16),
            jax.ShapeDtypeStruct((TOK, TOK, WIDTH), F32),
        ),
        in_specs=[pl.BlockSpec(memory_space=pltpu.SMEM)] + [whole] * 7,
        out_specs=(pl.BlockSpec(memory_space=pl.ANY), pl.BlockSpec(memory_space=pl.ANY)),
        scratch_shapes=[
            pltpu.VMEM((TOK, TOK, WIDTH), BF16),
            pltpu.VMEM((PART, WIDTH, WIDTH), BF16),
            pltpu.VMEM((WIDTH, TOK, WIDTH), BF16),
            pltpu.VMEM((COLS, ROWS, TOK, WIDTH), BF16),
            pltpu.VMEM((4, HALF * TOK, 4 * TOK), F32),
            pltpu.VMEM((HALF, COLS, TOK // 2, WIDTH), BF16),
            pltpu.VMEM((TOK, TOK, WIDTH), F32),
            pltpu.SemaphoreType.DMA,
            pltpu.SemaphoreType.DMA,
            pltpu.SemaphoreType.DMA((DEPTHS,)),
            pltpu.SemaphoreType.DMA((DEPTHS,)),
            pltpu.SemaphoreType.DMA((DEPTHS,)),
            pltpu.SemaphoreType.DMA,
            pltpu.SemaphoreType.DMA,
        ],
        compiler_params=pltpu.CompilerParams(collective_id=0, has_side_effects=True),
        name="exchange",
    )(mask, pair, wl, wr, wg, gain, bias, mask.reshape(DEPTHS, WIDTH))


CHUNK = 8


def update_kernel(q_ref, gate_ref, g_ref, b_ref, w_ref, out_ref, wide):
    @pl.when(pl.program_id(0) == 0)
    def _():
        wide[0] = jnp.broadcast_to(g_ref[...], (WIDTH, WIDTH)).T
        wide[1] = jnp.broadcast_to(b_ref[...], (WIDTH, WIDTH)).T

    turned = jnp.swapaxes(q_ref[...], 0, 1)
    for q in range(CHUNK):
        v = turned[q].astype(F32)
        v = v - jnp.mean(v, axis=0, keepdims=True)
        spread = jnp.mean(v * v, axis=0, keepdims=True)
        n = (v * lax.rsqrt(spread + EPS) * wide[0] + wide[1]).astype(BF16)
        o = lax.dot_general(n, w_ref[...], TN, preferred_element_type=F32)
        out_ref[0, q] = (gate_ref[0, q] * o[:TOK]).astype(BF16)
        out_ref[1, q] = (gate_ref[1, q] * o[TOK:]).astype(BF16)


def finish(q, gate, gain, bias, w):
    whole = lambda shape: pl.BlockSpec(shape, lambda i: (0,) * len(shape))
    part = pl.BlockSpec((2, CHUNK, TOK, WIDTH), lambda i: (0, i, 0, 0))
    return pl.pallas_call(
        update_kernel,
        out_shape=jax.ShapeDtypeStruct((2, TOK // 2, TOK, WIDTH), BF16),
        grid=(TOK // 2 // CHUNK,),
        in_specs=[
            pl.BlockSpec((WIDTH, CHUNK, WIDTH), lambda i: (0, i, 0)),
            part,
            whole((1, WIDTH)),
            whole((1, WIDTH)),
            whole((WIDTH, WIDTH)),
        ],
        out_specs=part,
        scratch_shapes=[pltpu.VMEM((2, WIDTH, WIDTH), F32)],
        name="finish",
    )(q, gate, gain, bias, w)


def shards(
    pair_rep,
    token_mask,
    in_gain,
    in_bias,
    left_weight,
    right_weight,
    gate_weight,
    out_gain,
    out_bias,
    out_weight,
):
    flat = lambda v: v.reshape(1, WIDTH)
    q, gate = exchange(
        token_mask, pair_rep, left_weight, right_weight, gate_weight, flat(in_gain), flat(in_bias)
    )
    out = finish(
        q, gate.reshape(2, TOK // 2, TOK, WIDTH), flat(out_gain), flat(out_bias), out_weight
    )
    return out.reshape(TOK, TOK, WIDTH)


def solution(mesh):
    placed = (P("row", "col", None), P(), P(), P(), P(), P(), P(), P(), P(), P())
    return jax.shard_map(
        shards, mesh=mesh, in_specs=placed, out_specs=P("row", "col", None), check_vma=False
    )
```

```python
import functools

import jax
import jax.numpy as jnp
from jax import lax
from jax.experimental import pallas as pl
from jax.experimental.pallas import tpu as pltpu
from jax.sharding import PartitionSpec as P

EPS = 1e-05
MESH = pl.DeviceIdType.MESH
F32 = jnp.float32
BF16 = jnp.bfloat16
NT = (((1,), (1,)), ((), ()))
TN = (((0,), (0,)), ((), ()))

ROWS = 16
COLS = 16
CHIPS = 8
DEPTHS = 8
TOK = 64
WIDTH = 128
HALF = 8


def sigmoid(v):
    return 0.5 * jnp.tanh(0.5 * v) + 0.5


SHIFTS = (4, 3, 5, 2, 6, 1, 7, 0)
PARTS = 2
LINES = TOK // 2
PART = LINES // PARTS


def shift_of(step):
    away = (step + 1) // 2
    return lax.rem(4 + (1 - 2 * lax.rem(step, 2)) * away, DEPTHS)


def exchange_kernel(
    mask_ref, x_ref, wl_ref, wr_ref, wg_ref, gain_ref, bias_ref, valid_ref,
    q_ref, gate_ref,
    n_buf, tr_buf, tl_buf, sr_buf, sl_buf, xr_buf, xl_buf, r_buf, p_buf, gate_buf,
    gate_sem, r_send, l_send, r_recv, l_recv, f_send, f_recv, p_send, p_recv,
):
    row, col = lax.axis_index("row"), lax.axis_index("col")
    core, half, chip, slot = lax.rem(row, 2), row // HALF, row // 2, lax.rem(row, HALF)
    depth, side = col // 2, lax.rem(col, 2)
    sibling = row + 1 - 2 * core
    channel = chip * COLS + col
    itself = half == core
    apart = jnp.logical_not(itself)

    barrier = pltpu.get_barrier_semaphore()

    def hello(to_row, to_col):
        pl.semaphore_signal(barrier, inc=1, device_id=(to_row, to_col), device_id_type=MESH)

    def greet(c, carry):
        for r in range(HALF):
            to_row = core * HALF + r
            pl.when(jnp.logical_not(jnp.logical_and(to_row == row, c == col)))(
                functools.partial(hello, to_row, c)
            )
        return carry

    lax.fori_loop(0, COLS, greet, 0)
    pl.when(apart)(functools.partial(hello, sibling, col))

    gain, bias = gain_ref[...], bias_ref[...]
    wide = 2 * WIDTH
    eye = lax.broadcasted_iota(jnp.int32, (wide, wide), 0)
    eye = jnp.where(eye == lax.broadcasted_iota(jnp.int32, (wide, wide), 1), 1.0, 0.0).astype(BF16)
    weight = jnp.concatenate(
        [
            lax.dot_general(eye, w[...], NT, preferred_element_type=F32).astype(BF16)
            for w in (wl_ref, wr_ref)
        ],
        1,
    )
    blank = jnp.zeros((TOK, WIDTH), BF16)
    lane = lax.broadcasted_iota(jnp.int32, (1, WIDTH), 1)
    held = valid_ref[pl.ds(depth, 1), :].astype(F32)
    near = jnp.where(side == 0, 1, 0) == jnp.where(lane < TOK, 1, 0)
    held = jnp.where(near, held, pltpu.roll(held, TOK, 1))

    left_half = lane < TOK

    def project(part):
        def eight(w, carry):
            for u in range(8):
                line = part * PART + 8 * w + u
                first, second = line + LINES * side, line + LINES * (1 - side)
                v = jnp.concatenate([x_ref[first], x_ref[second]], 0).astype(F32)
                v = v - jnp.mean(v, axis=-1, keepdims=True)
                spread = jnp.mean(v * v, axis=-1, keepdims=True)
                n = (v * lax.rsqrt(spread + EPS) * gain + bias).astype(BF16)
                n_buf[first] = n[:TOK]
                n_buf[second] = n[TOK:]
                empty = jnp.concatenate([blank, blank], 0)
                both = jnp.concatenate(
                    [jnp.concatenate([empty, n], 0), jnp.concatenate([n, empty], 0)], 1
                )
                d = lax.dot_general(weight, both, NT, preferred_element_type=F32)
                e = sigmoid(d[:WIDTH]) * d[WIDTH:]
                one = mask_ref[row * TOK + first].astype(F32)
                two = mask_ref[row * TOK + second].astype(F32)
                m = held * jnp.where(left_half, one, two)
                tr_buf[8 * w + u] = (e[:, :WIDTH] * m).astype(BF16)
                tl_buf[8 * w + u] = (e[:, WIDTH:] * m).astype(BF16)
            return carry

        lax.fori_loop(0, PART // 8, eight, 0)
        rows = pl.ds(part * PART, PART)
        sr_buf[:, rows, :] = jnp.swapaxes(tr_buf[...], 0, 1)
        sl_buf[:, rows, :] = jnp.swapaxes(tl_buf[...], 0, 1)

    chips = [lax.rem(chip + d, CHIPS) for d in range(CHIPS)]
    sides = [side, 1 - side]

    def send(buf, dst, send_sem, sem_of, part):
        rows = pl.ds(part * PART, PART)

        def send_to(step, d, to_col, alone):
            src = buf.at[chips[d] * COLS + to_col, rows]

            def remote():
                pltpu.make_async_remote_copy(
                    src_ref=src, dst_ref=dst, send_sem=send_sem, recv_sem=sem_of(step),
                    device_id=(chips[d] * 2 + half, to_col), device_id_type=MESH,
                ).start()

            def local():
                pltpu.make_async_copy(src, dst, sem_of(step)).start()

            if alone:
                pl.when(itself)(local)
                pl.when(apart)(remote)
            else:
                remote()

        far = lax.rem(depth + 4, DEPTHS) * 2
        for d in range(CHIPS):
            for e in range(2):
                send_to(0, d, far + sides[e], False)

        def pair(u, carry):
            down = lax.rem(depth + 4 - u, DEPTHS) * 2
            up = lax.rem(depth + 4 + u, DEPTHS) * 2
            for d in range(CHIPS):
                for e in range(2):
                    send_to(2 * u - 1, d, down + sides[e], False)
                    send_to(2 * u, d, up + sides[e], False)
            return carry

        lax.fori_loop(1, 4, pair, 0)
        for d in range(CHIPS):
            for e in range(2):
                send_to(7, d, depth * 2 + sides[e], d == 0 and e == 0)

    def send_right(part):
        dst = xr_buf.at[col, row, pl.ds(part * PART, PART)]
        send(sr_buf, dst, r_send, lambda step: r_recv.at[step], part)

    def send_left(part, carry):
        dst = xl_buf.at[col, slot, pl.ds(part * PART, PART)]
        send(sl_buf, dst, l_send, lambda step: l_recv.at[part], part)
        return carry

    project(0)
    pl.semaphore_wait(barrier, CHIPS * COLS)
    send_right(0)
    project(1)
    send_right(1)
    lax.fori_loop(0, PARTS, send_left, 0)

    def gates(u, carry):
        n = n_buf[pl.ds(4 * u, 4)].reshape(4 * TOK, WIDTH)
        gate = sigmoid(jnp.dot(n, wg_ref[...], preferred_element_type=F32))
        gate_buf[pl.ds(4 * u, 4)] = gate.reshape(4, TOK, WIDTH)
        return carry

    lax.fori_loop(0, TOK // 4, gates, 0)
    gate_copy = pltpu.make_async_copy(gate_buf, gate_ref, gate_sem)
    gate_copy.start()

    def forward(step):
        c = lax.rem(depth - shift_of(step) + DEPTHS, DEPTHS) * 2
        part = xr_buf.at[pl.ds(c, 2), pl.ds(core * HALF, HALF)]
        return part, pltpu.make_async_remote_copy(
            src_ref=part, dst_ref=part, send_sem=f_send.at[step], recv_sem=f_recv.at[step],
            device_id=(sibling, col), device_id_type=MESH,
        )

    def arrive(step, carry):
        part, copy = forward(step)
        pltpu.make_async_copy(part, part, r_recv.at[step]).wait()
        copy.start()
        return carry

    lax.fori_loop(0, DEPTHS, arrive, 0)

    def arrive_too(step, carry):
        forward(step)[1].wait_recv()
        return carry

    lax.fori_loop(0, DEPTHS, arrive_too, 0)

    def straight(even, odd, lanes):
        even, odd = even.astype(F32), odd.astype(F32)
        top = jnp.where(lanes, even, odd).astype(BF16)
        bot = pltpu.roll(jnp.where(lanes, odd, even), TOK, 1).astype(BF16)
        return top, bot

    def align_right(z, carry):
        for k in range(4):
            even, odd = (
                xr_buf[2 * z + e, 4 * k : 4 * k + 4].reshape(4 * LINES, WIDTH) for e in range(2)
            )
            top, bot = straight(even, odd, left_half)
            both = [v.reshape(4, LINES, WIDTH) for v in (top, bot)]
            r_buf[z, 4 * TOK * k : 4 * TOK * (k + 1), :] = jnp.concatenate(both, 1).reshape(
                4 * TOK, WIDTH
            )
        return carry

    lax.fori_loop(0, DEPTHS, align_right, 0)

    targets = [
        lax.rem(depth + shift, DEPTHS) * 2 + sides[e] for shift in SHIFTS for e in range(2)
    ]

    def multiply(part):
        rows = pl.ds(part * PART, PART)
        arrived = xl_buf.at[:, :, rows]
        pltpu.make_async_copy(arrived, arrived, l_recv.at[part]).wait()
        own = []
        for z in range(DEPTHS):
            even, odd = (
                xl_buf[2 * z + e, :, rows, :].reshape(HALF * PART, WIDTH) for e in range(2)
            )
            both = [v.reshape(HALF, PART, WIDTH) for v in straight(even, odd, left_half)]
            own.append(jnp.concatenate(both, 1).reshape(HALF * 2 * PART, WIDTH))
        own = jnp.concatenate(own, 1)

        def block(n, carry):
            start = pl.multiple_of(n * 4 * TOK, 4 * TOK)
            others = jnp.concatenate([r_buf[z, pl.ds(start, 4 * TOK), :] for z in range(DEPTHS)], 1)
            v = lax.dot_general(own, others, NT, preferred_element_type=F32)
            for r in range(HALF):
                for m in range(2):
                    w = v[2 * PART * r : 2 * PART * (r + 1), m * WIDTH : (m + 1) * WIDTH]
                    top, bot = w[:PART], w[PART:]
                    even = jnp.where(left_half, top, pltpu.roll(bot, TOK, 1))
                    odd = jnp.where(left_half, pltpu.roll(top, TOK, 1), bot)
                    p_buf[part, r, 4 * n + 2 * m] = even.astype(BF16)
                    p_buf[part, r, 4 * n + 2 * m + 1] = odd.astype(BF16)
            return carry

        lax.fori_loop(0, 4, block, 0)

    def give(part):
        def one_row(u, carry):
            r = lax.rem(slot + u, HALF)
            to_row = core * HALF + r
            dst = q_ref.at[channel, pl.ds(part * PART, PART)]
            for k, to_col in enumerate(targets):
                src = p_buf.at[part, r, to_col]

                def remote(src=src, to_col=to_col):
                    pltpu.make_async_remote_copy(
                        src_ref=src, dst_ref=dst,
                        send_sem=p_send.at[part], recv_sem=p_recv.at[part],
                        device_id=(to_row, to_col), device_id_type=MESH,
                    ).start()

                def local(src=src):
                    pltpu.make_async_copy(src, dst, p_recv.at[part]).start()

                if SHIFTS[k // 2] == 0 and k % 2 == 0:
                    here = to_row == row
                    pl.when(here)(local)
                    pl.when(jnp.logical_not(here))(remote)
                else:
                    remote()
            return carry

        lax.fori_loop(0, HALF, one_row, 0)

    def product(part, carry):
        multiply(part)
        give(part)
        return carry

    lax.fori_loop(0, PARTS, product, 0)

    gate_copy.wait()

    def drain(step, carry):
        forward(step)[1].wait_send()
        return carry

    lax.fori_loop(0, DEPTHS, drain, 0)

    def finished(n):
        for buf, sem in ((sr_buf, r_send), (sl_buf, l_send)):
            sent = buf.at[pl.ds(0, n)]
            pltpu.make_async_copy(sent, sent, sem).wait()
        for part in range(PARTS):
            given = q_ref.at[pl.ds(0, n), pl.ds(part * PART, PART)]
            pltpu.make_async_copy(given, given, p_send.at[part]).wait()

    pl.when(itself)(functools.partial(finished, WIDTH - 1))
    pl.when(apart)(functools.partial(finished, WIDTH))
    for part in range(PARTS):
        come = q_ref.at[:, pl.ds(part * PART, PART)]
        pltpu.make_async_copy(come, come, p_recv.at[part]).wait()


def exchange(mask, pair, wl, wr, wg, gain, bias):
    whole = pl.BlockSpec(memory_space=pltpu.VMEM)
    return pl.pallas_call(
        exchange_kernel,
        out_shape=(
            jax.ShapeDtypeStruct((WIDTH, TOK // 2, WIDTH), BF16),
            jax.ShapeDtypeStruct((TOK, TOK, WIDTH), F32),
        ),
        in_specs=[pl.BlockSpec(memory_space=pltpu.SMEM)] + [whole] * 7,
        out_specs=(pl.BlockSpec(memory_space=pl.ANY), pl.BlockSpec(memory_space=pl.ANY)),
        scratch_shapes=[
            pltpu.VMEM((TOK, TOK, WIDTH), BF16),
            pltpu.VMEM((PART, WIDTH, WIDTH), BF16),
            pltpu.VMEM((PART, WIDTH, WIDTH), BF16),
            pltpu.VMEM((WIDTH, LINES, WIDTH), BF16),
            pltpu.VMEM((WIDTH, LINES, WIDTH), BF16),
            pltpu.VMEM((COLS, ROWS, LINES, WIDTH), BF16),
            pltpu.VMEM((COLS, HALF, LINES, WIDTH), BF16),
            pltpu.VMEM((DEPTHS, ROWS * TOK, WIDTH), BF16),
            pltpu.VMEM((PARTS, HALF, COLS, PART, WIDTH), BF16),
            pltpu.VMEM((TOK, TOK, WIDTH), F32),
            pltpu.SemaphoreType.DMA,
            pltpu.SemaphoreType.DMA,
            pltpu.SemaphoreType.DMA,
            pltpu.SemaphoreType.DMA((DEPTHS,)),
            pltpu.SemaphoreType.DMA((PARTS,)),
            pltpu.SemaphoreType.DMA((DEPTHS,)),
            pltpu.SemaphoreType.DMA((DEPTHS,)),
            pltpu.SemaphoreType.DMA((PARTS,)),
            pltpu.SemaphoreType.DMA((PARTS,)),
        ],
        compiler_params=pltpu.CompilerParams(collective_id=0, has_side_effects=True),
        name="exchange",
    )(mask, pair, wl, wr, wg, gain, bias, mask.reshape(DEPTHS, WIDTH))


CHUNK = 8


def update_kernel(q_ref, gate_ref, g_ref, b_ref, w_ref, out_ref, wide):
    @pl.when(pl.program_id(0) == 0)
    def _():
        wide[0] = jnp.broadcast_to(g_ref[...], (WIDTH, WIDTH)).T
        wide[1] = jnp.broadcast_to(b_ref[...], (WIDTH, WIDTH)).T

    turned = jnp.swapaxes(q_ref[...], 0, 1)
    for q in range(CHUNK):
        v = turned[q].astype(F32)
        v = v - jnp.mean(v, axis=0, keepdims=True)
        spread = jnp.mean(v * v, axis=0, keepdims=True)
        n = (v * lax.rsqrt(spread + EPS) * wide[0] + wide[1]).astype(BF16)
        o = lax.dot_general(n, w_ref[...], TN, preferred_element_type=F32)
        out_ref[0, q] = (gate_ref[0, q] * o[:TOK]).astype(BF16)
        out_ref[1, q] = (gate_ref[1, q] * o[TOK:]).astype(BF16)


def finish(q, gate, gain, bias, w):
    whole = lambda shape: pl.BlockSpec(shape, lambda i: (0,) * len(shape))
    part = pl.BlockSpec((2, CHUNK, TOK, WIDTH), lambda i: (0, i, 0, 0))
    return pl.pallas_call(
        update_kernel,
        out_shape=jax.ShapeDtypeStruct((2, TOK // 2, TOK, WIDTH), BF16),
        grid=(TOK // 2 // CHUNK,),
        in_specs=[
            pl.BlockSpec((WIDTH, CHUNK, WIDTH), lambda i: (0, i, 0)),
            part,
            whole((1, WIDTH)),
            whole((1, WIDTH)),
            whole((WIDTH, WIDTH)),
        ],
        out_specs=part,
        scratch_shapes=[pltpu.VMEM((2, WIDTH, WIDTH), F32)],
        name="finish",
    )(q, gate, gain, bias, w)


def shards(
    pair_rep,
    token_mask,
    in_gain,
    in_bias,
    left_weight,
    right_weight,
    gate_weight,
    out_gain,
    out_bias,
    out_weight,
):
    flat = lambda v: v.reshape(1, WIDTH)
    q, gate = exchange(
        token_mask, pair_rep, left_weight, right_weight, gate_weight, flat(in_gain), flat(in_bias)
    )
    out = finish(
        q, gate.reshape(2, TOK // 2, TOK, WIDTH), flat(out_gain), flat(out_bias), out_weight
    )
    return out.reshape(TOK, TOK, WIDTH)


def solution(mesh):
    placed = (P("row", "col", None), P(), P(), P(), P(), P(), P(), P(), P(), P())
    return jax.shard_map(
        shards, mesh=mesh, in_specs=placed, out_specs=P("row", "col", None), check_vma=False
    )
```

```python
import functools

import jax
import jax.numpy as jnp
from jax import lax
from jax.experimental import pallas as pl
from jax.experimental.pallas import tpu as pltpu
from jax.sharding import PartitionSpec as P

EPS = 1e-05
MESH = pl.DeviceIdType.MESH
F32 = jnp.float32
BF16 = jnp.bfloat16
NT = (((1,), (1,)), ((), ()))
TN = (((0,), (0,)), ((), ()))

ROWS = 16
COLS = 16
CHIPS = 8
DEPTHS = 8
TOK = 64
WIDTH = 128
LIMIT = 60 * 1024 * 1024
HALF = 8


def sigmoid(v):
    return 0.5 * jnp.tanh(0.5 * v) + 0.5


REACH = 4
PARTS = 2
LINES = TOK // 2
PART = LINES // PARTS


def exchange_kernel(
    mask_ref, x_ref, wl_ref, wr_ref, wg_ref, gain_ref, bias_ref, valid_ref,
    og_ref, ob_ref, ow_ref,
    out_ref,
    n_buf, tr_buf, tl_buf, sr_buf, sl_buf, xr_buf, xl_buf, r_buf, p_buf, q_ref, gate_buf, wide_buf, out_buf,
    kept, given_buf, taken,
    out_sem, r_send, l_send, r_recv, l_recv, f_send, f_recv, p_send, p_recv,
    e_send, e_recv,
):
    row, col = lax.axis_index("row"), lax.axis_index("col")
    core, half, chip, slot = lax.rem(row, 2), row // HALF, row // 2, lax.rem(row, HALF)
    depth, side = col // 2, lax.rem(col, 2)
    sibling = row + 1 - 2 * core
    above = lax.rem(depth + 1, DEPTHS) * 2 + side
    below = lax.rem(depth + DEPTHS - 1, DEPTHS) * 2 + side
    channels = (chip * COLS + col, chip * COLS + below)
    itself = half == core
    apart = jnp.logical_not(itself)

    barrier = pltpu.get_barrier_semaphore()

    def hello(to_row, to_col):
        pl.semaphore_signal(barrier, inc=1, device_id=(to_row, to_col), device_id_type=MESH)

    def greet(t, carry):
        to_col = lax.rem(col + t, COLS)
        for r in range(HALF):
            hello(core * HALF + r, to_col)
        return carry

    lax.fori_loop(1, COLS, greet, 0)
    for r in range(HALF):
        pl.when(core * HALF + r != row)(functools.partial(hello, core * HALF + r, col))

    @pl.when(apart)
    def _():
        hello(sibling, col)
        hello(row, above)
        hello(row, below)


    gain, bias = gain_ref[...], bias_ref[...]
    wide = 2 * WIDTH
    eye = lax.broadcasted_iota(jnp.int32, (wide, wide), 0)
    eye = jnp.where(eye == lax.broadcasted_iota(jnp.int32, (wide, wide), 1), 1.0, 0.0).astype(BF16)
    weight = jnp.concatenate(
        [
            lax.dot_general(eye, w[...], NT, preferred_element_type=F32).astype(BF16)
            for w in (wl_ref, wr_ref)
        ],
        1,
    )
    blank = jnp.zeros((TOK, WIDTH), BF16)
    lane = lax.broadcasted_iota(jnp.int32, (1, WIDTH), 1)
    held = valid_ref[pl.ds(depth, 1), :].astype(F32)
    near = jnp.where(side == 0, 1, 0) == jnp.where(lane < TOK, 1, 0)
    held = jnp.where(near, held, pltpu.roll(held, TOK, 1))

    left_half = lane < TOK

    def project(part):
        def eight(w, carry):
            for u in range(8):
                line = part * PART + 8 * w + u
                first, second = line + LINES * side, line + LINES * (1 - side)
                v = jnp.concatenate([x_ref[first], x_ref[second]], 0).astype(F32)
                v = v - jnp.mean(v, axis=-1, keepdims=True)
                spread = jnp.mean(v * v, axis=-1, keepdims=True)
                n = (v * lax.rsqrt(spread + EPS) * gain + bias).astype(BF16)
                n_buf[first] = n[:TOK]
                n_buf[second] = n[TOK:]
                empty = jnp.concatenate([blank, blank], 0)
                both = jnp.concatenate(
                    [jnp.concatenate([empty, n], 0), jnp.concatenate([n, empty], 0)], 1
                )
                d = lax.dot_general(weight, both, NT, preferred_element_type=F32)
                e = sigmoid(d[:WIDTH]) * d[WIDTH:]
                one = mask_ref[row * TOK + first].astype(F32)
                two = mask_ref[row * TOK + second].astype(F32)
                m = held * jnp.where(left_half, one, two)
                tr_buf[8 * w + u] = (e[:, :WIDTH] * m).astype(BF16)
                tl_buf[8 * w + u] = (e[:, WIDTH:] * m).astype(BF16)
            return carry

        lax.fori_loop(0, PART // 8, eight, 0)
        rows = pl.ds(part * PART, PART)
        sr_buf[:, rows, :] = jnp.swapaxes(tr_buf[...], 0, 1)
        sl_buf[:, rows, :] = jnp.swapaxes(tl_buf[...], 0, 1)

    chips = [lax.rem(chip + d, CHIPS) for d in range(CHIPS)]
    sides = [side, 1 - side]

    def send(buf, dst_of, send_sem, sem_of, part):
        rows = pl.ds(part * PART, PART)

        def send_to(role, reach, d, e, alone):
            plane = lax.rem(depth + (reach if role == 0 else DEPTHS - reach), DEPTHS)
            owner = plane if role == 0 else lax.rem(plane + DEPTHS - 1, DEPTHS)
            src = buf.at[chips[d] * COLS + owner * 2 + sides[e], rows]
            step = role * REACH + reach
            dst = dst_of(step)

            def remote():
                pltpu.make_async_remote_copy(
                    src_ref=src, dst_ref=dst, send_sem=send_sem, recv_sem=sem_of(step),
                    device_id=(chips[d] * 2 + half, plane * 2 + sides[e]), device_id_type=MESH,
                ).start()

            def local():
                pltpu.make_async_copy(src, dst, sem_of(step)).start()

            if alone:
                pl.when(itself)(local)
                pl.when(apart)(remote)
            else:
                remote()

        def far(u, carry):
            for d in range(CHIPS):
                for e in range(2):
                    for role in range(2):
                        send_to(role, REACH - 1 - u, d, e, False)
            return carry

        lax.fori_loop(0, REACH - 1, far, 0)
        for d in range(CHIPS):
            for e in range(2):
                for role in range(2):
                    send_to(role, 0, d, e, d == 0 and e == 0)

    def send_right(part):
        rows = pl.ds(part * PART, PART)
        send(
            sr_buf, lambda step: xr_buf.at[step, side, row, rows],
            r_send, lambda step: r_recv.at[step], part,
        )

    def send_left(part, carry):
        rows = pl.ds(part * PART, PART)
        send(
            sl_buf, lambda step: xl_buf.at[step, side, slot, rows],
            l_send, lambda step: l_recv.at[part], part,
        )
        return carry

    project(0)

    @pl.when(itself)
    def _():
        pl.semaphore_wait(barrier, CHIPS * COLS)

    @pl.when(apart)
    def _():
        pl.semaphore_wait(barrier, CHIPS * COLS + 2)

    send_right(0)
    project(1)
    send_right(1)
    lax.fori_loop(0, PARTS, send_left, 0)

    def gates(u, carry):
        n = n_buf[pl.ds(4 * u, 4)].reshape(4 * TOK, WIDTH)
        gate = sigmoid(jnp.dot(n, wg_ref[...], preferred_element_type=F32))
        gate_buf[pl.ds(4 * u, 4)] = gate.reshape(4, TOK, WIDTH)
        return carry

    lax.fori_loop(0, TOK // 4, gates, 0)
    wide_buf[0] = jnp.broadcast_to(og_ref[...], (WIDTH, WIDTH)).T
    wide_buf[1] = jnp.broadcast_to(ob_ref[...], (WIDTH, WIDTH)).T

    def forward(step):
        part = xr_buf.at[step, :, pl.ds(core * HALF, HALF)]
        return part, pltpu.make_async_remote_copy(
            src_ref=part, dst_ref=part, send_sem=f_send.at[step], recv_sem=f_recv.at[step],
            device_id=(sibling, col), device_id_type=MESH,
        )

    def arrive(step, carry):
        part, copy = forward(step)
        pltpu.make_async_copy(part, part, r_recv.at[step]).wait()
        copy.start()
        return carry

    lax.fori_loop(0, DEPTHS, arrive, 0)

    def arrive_too(step, carry):
        forward(step)[1].wait_recv()
        return carry

    lax.fori_loop(0, DEPTHS, arrive_too, 0)

    def straight(even, odd, lanes):
        even, odd = even.astype(F32), odd.astype(F32)
        top = jnp.where(lanes, even, odd).astype(BF16)
        bot = pltpu.roll(jnp.where(lanes, odd, even), TOK, 1).astype(BF16)
        return top, bot

    def align_right(z, carry):
        for k in range(4):
            even, odd = (
                xr_buf[z, e, 4 * k : 4 * k + 4].reshape(4 * LINES, WIDTH) for e in range(2)
            )
            top, bot = straight(even, odd, left_half)
            both = [v.reshape(4, LINES, WIDTH) for v in (top, bot)]
            r_buf[z, 4 * TOK * k : 4 * TOK * (k + 1), :] = jnp.concatenate(both, 1).reshape(
                4 * TOK, WIDTH
            )
        return carry

    lax.fori_loop(0, DEPTHS, align_right, 0)

    def plane_of(role, own, t):
        up = t if own else -1 - t
        return lax.rem(depth + (up if role == 1 else -up) + DEPTHS, DEPTHS)

    def hand(part, role):
        return pltpu.make_async_remote_copy(
            src_ref=given_buf.at[part, role], dst_ref=taken.at[part, 1 - role],
            send_sem=e_send.at[part, role], recv_sem=e_recv.at[part, 1 - role],
            device_id=(row, above if role == 0 else below), device_id_type=MESH,
        )

    def multiply(part, carry):
        rows = pl.ds(part * PART, PART)
        arrived = xl_buf.at[:, :, :, rows]
        pltpu.make_async_copy(arrived, arrived, l_recv.at[part]).wait()
        owns = []
        for role in range(2):
            own = []
            for z in range(role * REACH, (role + 1) * REACH):
                even, odd = (xl_buf[z, e, :, rows, :].reshape(HALF * PART, WIDTH) for e in range(2))
                both = [v.reshape(HALF, PART, WIDTH) for v in straight(even, odd, left_half)]
                own.append(jnp.concatenate(both, 1).reshape(HALF * 2 * PART, WIDTH))
            owns.append(jnp.concatenate(own, 1))
        for own_columns in (False, True):
            for role in range(2):
                for t in range(0, REACH, 2):
                    starts = [
                        pl.multiple_of(plane_of(role, own_columns, t + k) * 2 * TOK, 2 * TOK)
                        for k in range(2)
                    ]
                    others = jnp.concatenate(
                        [
                            jnp.concatenate(
                                [r_buf[z, pl.ds(start, 2 * TOK), :] for start in starts], 0
                            )
                            for z in range(role * REACH, (role + 1) * REACH)
                        ],
                        1,
                    )
                    v = lax.dot_general(owns[role], others, NT, preferred_element_type=F32)
                    for k in range(2):
                        w = v[:, k * WIDTH : (k + 1) * WIDTH]
                        if own_columns:
                            kept[part, role, t + k] = w
                        else:
                            given_buf[part, role, t + k] = w.astype(BF16)
                if not own_columns:
                    hand(part, role).start()
        return carry

    lax.fori_loop(0, PARTS, multiply, 0)

    def give(part, carry):
        for role in range(2):
            hand(part, 1 - role).wait_recv()
        for t in range(REACH - 1, -1, -1):
            for role in range(2):
                w = kept[part, role, t] + taken[part, role, t].astype(F32)
                for r in range(HALF):
                    top = w[2 * PART * r : 2 * PART * r + PART]
                    bot = w[2 * PART * r + PART : 2 * PART * (r + 1)]
                    even = jnp.where(left_half, top, pltpu.roll(bot, TOK, 1))
                    odd = jnp.where(left_half, pltpu.roll(top, TOK, 1), bot)
                    p_buf[part, role, t, 0, r] = even.astype(BF16)
                    p_buf[part, role, t, 1, r] = odd.astype(BF16)
                plane = plane_of(role, True, t)
                dst = q_ref.at[channels[role], pl.ds(part * PART, PART)]
                for u in range(HALF):
                    r = lax.rem(slot + u, HALF)
                    for e in range(2):
                        src = p_buf.at[part, role, t, sides[e], r]

                        def remote(src=src, dst=dst, r=r, plane=plane, e=e):
                            pltpu.make_async_remote_copy(
                                src_ref=src, dst_ref=dst,
                                send_sem=p_send.at[part], recv_sem=p_recv.at[part],
                                device_id=(core * HALF + r, plane * 2 + sides[e]),
                                device_id_type=MESH,
                            ).start()

                        def local(src=src, dst=dst):
                            pltpu.make_async_copy(src, dst, p_recv.at[part]).start()

                        if t == 0 and u == 0 and e == 0:
                            pl.when(itself)(local)
                            pl.when(apart)(remote)
                        else:
                            remote()
        return carry

    lax.fori_loop(0, PARTS, give, 0)

    def put(part):
        rows = pl.ds(part * PART, PART)
        return pltpu.make_async_copy(out_buf.at[:, rows], out_ref.at[:, rows], out_sem.at[part])

    def finish(part, carry):
        come = q_ref.at[:, pl.ds(part * PART, PART)]
        pltpu.make_async_copy(come, come, p_recv.at[part]).wait()
        turned = jnp.swapaxes(q_ref[:, pl.ds(part * PART, PART), :], 0, 1)
        for u in range(PART):
            v = turned[u].astype(F32)
            v = v - jnp.mean(v, axis=0, keepdims=True)
            spread = jnp.mean(v * v, axis=0, keepdims=True)
            n = (v * lax.rsqrt(spread + EPS) * wide_buf[0] + wide_buf[1]).astype(BF16)
            o = lax.dot_general(n, ow_ref[...], TN, preferred_element_type=F32)
            line = part * PART + u
            out_buf[0, line] = (gate_buf[line] * o[:TOK]).astype(BF16)
            out_buf[1, line] = (gate_buf[LINES + line] * o[TOK:]).astype(BF16)
        put(part).start()
        return carry

    lax.fori_loop(0, PARTS, finish, 0)

    def drain(step, carry):
        forward(step)[1].wait_send()
        return carry

    lax.fori_loop(0, DEPTHS, drain, 0)

    for part in range(PARTS):
        for role in range(2):
            hand(part, role).wait_send()

    def finished(n):
        for buf, sem in ((sr_buf, r_send), (sl_buf, l_send)):
            sent = buf.at[pl.ds(0, n)]
            pltpu.make_async_copy(sent, sent, sem).wait()
        for part in range(PARTS):
            given = q_ref.at[pl.ds(0, n), pl.ds(part * PART, PART)]
            pltpu.make_async_copy(given, given, p_send.at[part]).wait()

    pl.when(itself)(functools.partial(finished, WIDTH - 2))
    pl.when(apart)(functools.partial(finished, WIDTH))
    for part in range(PARTS):
        put(part).wait()


def exchange(mask, pair, wl, wr, wg, gain, bias, og, ob, ow):
    whole = pl.BlockSpec(memory_space=pltpu.VMEM)
    return pl.pallas_call(
        exchange_kernel,
        out_shape=jax.ShapeDtypeStruct((2, LINES, TOK, WIDTH), BF16),
        in_specs=[pl.BlockSpec(memory_space=pltpu.SMEM)] + [whole] * 10,
        out_specs=pl.BlockSpec(memory_space=pl.ANY),
        scratch_shapes=[
            pltpu.VMEM((TOK, TOK, WIDTH), BF16),
            pltpu.VMEM((PART, WIDTH, WIDTH), BF16),
            pltpu.VMEM((PART, WIDTH, WIDTH), BF16),
            pltpu.VMEM((WIDTH, LINES, WIDTH), BF16),
            pltpu.VMEM((WIDTH, LINES, WIDTH), BF16),
            pltpu.VMEM((2 * REACH, 2, ROWS, LINES, WIDTH), BF16),
            pltpu.VMEM((2 * REACH, 2, HALF, LINES, WIDTH), BF16),
            pltpu.VMEM((DEPTHS, ROWS * TOK, WIDTH), BF16),
            pltpu.VMEM((PARTS, 2, REACH, 2, HALF, PART, WIDTH), BF16),
            pltpu.VMEM((WIDTH, LINES, WIDTH), BF16),
            pltpu.VMEM((TOK, TOK, WIDTH), F32),
            pltpu.VMEM((2, WIDTH, WIDTH), F32),
            pltpu.VMEM((2, LINES, TOK, WIDTH), BF16),
            pltpu.VMEM((PARTS, 2, REACH, HALF * 2 * PART, WIDTH), F32),
            pltpu.VMEM((PARTS, 2, REACH, HALF * 2 * PART, WIDTH), BF16),
            pltpu.VMEM((PARTS, 2, REACH, HALF * 2 * PART, WIDTH), BF16),
            pltpu.SemaphoreType.DMA((PARTS,)),
            pltpu.SemaphoreType.DMA,
            pltpu.SemaphoreType.DMA,
            pltpu.SemaphoreType.DMA((DEPTHS,)),
            pltpu.SemaphoreType.DMA((PARTS,)),
            pltpu.SemaphoreType.DMA((DEPTHS,)),
            pltpu.SemaphoreType.DMA((DEPTHS,)),
            pltpu.SemaphoreType.DMA((PARTS,)),
            pltpu.SemaphoreType.DMA((PARTS,)),
            pltpu.SemaphoreType.DMA((PARTS, 2)),
            pltpu.SemaphoreType.DMA((PARTS, 2)),
        ],
        compiler_params=pltpu.CompilerParams(
            collective_id=0, has_side_effects=True, vmem_limit_bytes=LIMIT
        ),
        name="exchange",
    )(mask, pair, wl, wr, wg, gain, bias, mask.reshape(DEPTHS, WIDTH), og, ob, ow)


def shards(
    pair_rep,
    token_mask,
    in_gain,
    in_bias,
    left_weight,
    right_weight,
    gate_weight,
    out_gain,
    out_bias,
    out_weight,
):
    flat = lambda v: v.reshape(1, WIDTH)
    out = exchange(
        token_mask,
        pair_rep,
        left_weight,
        right_weight,
        gate_weight,
        flat(in_gain),
        flat(in_bias),
        flat(out_gain),
        flat(out_bias),
        out_weight,
    )
    return out.reshape(TOK, TOK, WIDTH)


def solution(mesh):
    placed = (P("row", "col", None), P(), P(), P(), P(), P(), P(), P(), P(), P())
    return jax.shard_map(
        shards, mesh=mesh, in_specs=placed, out_specs=P("row", "col", None), check_vma=False
    )
```

```python
import functools

import jax
import jax.numpy as jnp
from jax import lax
from jax.experimental import pallas as pl
from jax.experimental.pallas import tpu as pltpu
from jax.sharding import PartitionSpec as P

EPS = 1e-05
MESH = pl.DeviceIdType.MESH
F32 = jnp.float32
BF16 = jnp.bfloat16
NT = (((1,), (1,)), ((), ()))
TN = (((0,), (0,)), ((), ()))

ROWS = 16
COLS = 16
CHIPS = 8
DEPTHS = 8
TOK = 64
WIDTH = 128
LIMIT = 60 * 1024 * 1024
HALF = 8


def sigmoid(v):
    return 0.5 * jnp.tanh(0.5 * v) + 0.5


REACH = 4
PARTS = 2
LINES = TOK // 2
PART = LINES // PARTS


def exchange_kernel(
    mask_hbm, x_hbm, wl_hbm, wr_hbm, wg_hbm, gain_hbm, bias_hbm, valid_hbm,
    og_hbm, ob_hbm, ow_hbm,
    out_ref,
    mask_ref, x_ref, wl_ref, wr_ref, wg_ref, gain_ref, bias_ref, valid_ref,
    og_ref, ob_ref, ow_ref, in_sem,
    n_buf, tr_buf, tl_buf, sr_buf, sl_buf, xr_buf, xl_buf, r_buf, p_buf, q_ref, gate_buf, wide_buf, out_buf,
    kept, given_buf, taken,
    out_sem, r_send, l_send, r_recv, l_recv, f_send, f_recv, p_send, p_recv,
    e_send, e_recv,
):
    row, col = lax.axis_index("row"), lax.axis_index("col")
    core, half, chip, slot = lax.rem(row, 2), row // HALF, row // 2, lax.rem(row, HALF)
    depth, side = col // 2, lax.rem(col, 2)
    sibling = row + 1 - 2 * core
    above = lax.rem(depth + 1, DEPTHS) * 2 + side
    below = lax.rem(depth + DEPTHS - 1, DEPTHS) * 2 + side
    channels = (chip * COLS + col, chip * COLS + below)
    itself = half == core
    apart = jnp.logical_not(itself)

    loads = [
        pltpu.make_async_copy(src, dst, in_sem.at[k])
        for k, (src, dst) in enumerate(
            (
                (wl_hbm, wl_ref),
                (wr_hbm, wr_ref),
                (x_hbm, x_ref),
                (gain_hbm, gain_ref),
                (bias_hbm, bias_ref),
                (valid_hbm, valid_ref),
                (mask_hbm, mask_ref),
                (wg_hbm, wg_ref),
                (og_hbm, og_ref),
                (ob_hbm, ob_ref),
                (ow_hbm, ow_ref),
            )
        )
    ]
    for load in loads:
        load.start()

    barrier = pltpu.get_barrier_semaphore()

    def hello(to_row, to_col):
        pl.semaphore_signal(barrier, inc=1, device_id=(to_row, to_col), device_id_type=MESH)

    def greet(t, carry):
        to_col = lax.rem(col + t, COLS)
        for r in range(HALF):
            hello(core * HALF + r, to_col)
        return carry

    lax.fori_loop(1, COLS, greet, 0)
    for r in range(HALF):
        pl.when(core * HALF + r != row)(functools.partial(hello, core * HALF + r, col))

    @pl.when(apart)
    def _():
        hello(sibling, col)
        hello(row, above)
        hello(row, below)


    for load in loads:
        load.wait()

    gain, bias = gain_ref[...], bias_ref[...]
    wide = 2 * WIDTH
    eye = lax.broadcasted_iota(jnp.int32, (wide, wide), 0)
    eye = jnp.where(eye == lax.broadcasted_iota(jnp.int32, (wide, wide), 1), 1.0, 0.0).astype(BF16)
    weight = jnp.concatenate(
        [
            lax.dot_general(eye, w[...], NT, preferred_element_type=F32).astype(BF16)
            for w in (wl_ref, wr_ref)
        ],
        1,
    )
    blank = jnp.zeros((TOK, WIDTH), BF16)
    lane = lax.broadcasted_iota(jnp.int32, (1, WIDTH), 1)
    held = valid_ref[pl.ds(depth, 1), :].astype(F32)
    near = jnp.where(side == 0, 1, 0) == jnp.where(lane < TOK, 1, 0)
    held = jnp.where(near, held, pltpu.roll(held, TOK, 1))

    left_half = lane < TOK

    def project(part):
        def eight(w, carry):
            for u in range(8):
                line = part * PART + 8 * w + u
                first, second = line + LINES * side, line + LINES * (1 - side)
                v = jnp.concatenate([x_ref[first], x_ref[second]], 0).astype(F32)
                v = v - jnp.mean(v, axis=-1, keepdims=True)
                spread = jnp.mean(v * v, axis=-1, keepdims=True)
                n = (v * lax.rsqrt(spread + EPS) * gain + bias).astype(BF16)
                n_buf[first] = n[:TOK]
                n_buf[second] = n[TOK:]
                empty = jnp.concatenate([blank, blank], 0)
                both = jnp.concatenate(
                    [jnp.concatenate([empty, n], 0), jnp.concatenate([n, empty], 0)], 1
                )
                d = lax.dot_general(weight, both, NT, preferred_element_type=F32)
                e = sigmoid(d[:WIDTH]) * d[WIDTH:]
                one = mask_ref[row * TOK + first].astype(F32)
                two = mask_ref[row * TOK + second].astype(F32)
                m = held * jnp.where(left_half, one, two)
                tr_buf[8 * w + u] = (e[:, :WIDTH] * m).astype(BF16)
                tl_buf[8 * w + u] = (e[:, WIDTH:] * m).astype(BF16)
            return carry

        lax.fori_loop(0, PART // 8, eight, 0)
        rows = pl.ds(part * PART, PART)
        sr_buf[:, rows, :] = jnp.swapaxes(tr_buf[...], 0, 1)
        sl_buf[:, rows, :] = jnp.swapaxes(tl_buf[...], 0, 1)

    chips = [lax.rem(chip + d, CHIPS) for d in range(CHIPS)]
    sides = [side, 1 - side]

    def send(buf, dst_of, send_sem, sem_of, part):
        rows = pl.ds(part * PART, PART)

        def send_to(role, reach, d, e, alone):
            plane = lax.rem(depth + (reach if role == 0 else DEPTHS - reach), DEPTHS)
            owner = plane if role == 0 else lax.rem(plane + DEPTHS - 1, DEPTHS)
            src = buf.at[chips[d] * COLS + owner * 2 + sides[e], rows]
            step = role * REACH + reach
            dst = dst_of(step)

            def remote():
                pltpu.make_async_remote_copy(
                    src_ref=src, dst_ref=dst, send_sem=send_sem, recv_sem=sem_of(step),
                    device_id=(chips[d] * 2 + half, plane * 2 + sides[e]), device_id_type=MESH,
                ).start()

            def local():
                pltpu.make_async_copy(src, dst, sem_of(step)).start()

            if alone:
                pl.when(itself)(local)
                pl.when(apart)(remote)
            else:
                remote()

        def far(u, carry):
            for d in range(CHIPS):
                for e in range(2):
                    for role in range(2):
                        send_to(role, REACH - 1 - u, d, e, False)
            return carry

        lax.fori_loop(0, REACH - 1, far, 0)
        for d in range(CHIPS):
            for e in range(2):
                for role in range(2):
                    send_to(role, 0, d, e, d == 0 and e == 0)

    def send_right(part):
        rows = pl.ds(part * PART, PART)
        send(
            sr_buf, lambda step: xr_buf.at[step, side, row, rows],
            r_send, lambda step: r_recv.at[step], part,
        )

    def send_left(part, carry):
        rows = pl.ds(part * PART, PART)
        send(
            sl_buf, lambda step: xl_buf.at[step, side, slot, rows],
            l_send, lambda step: l_recv.at[part], part,
        )
        return carry

    project(0)

    @pl.when(itself)
    def _():
        pl.semaphore_wait(barrier, CHIPS * COLS)

    @pl.when(apart)
    def _():
        pl.semaphore_wait(barrier, CHIPS * COLS + 2)

    send_right(0)
    project(1)
    send_right(1)
    lax.fori_loop(0, PARTS, send_left, 0)

    def gates(u, carry):
        n = n_buf[pl.ds(4 * u, 4)].reshape(4 * TOK, WIDTH)
        gate = sigmoid(jnp.dot(n, wg_ref[...], preferred_element_type=F32))
        gate_buf[pl.ds(4 * u, 4)] = gate.reshape(4, TOK, WIDTH)
        return carry

    lax.fori_loop(0, TOK // 4, gates, 0)
    wide_buf[0] = jnp.broadcast_to(og_ref[...], (WIDTH, WIDTH)).T
    wide_buf[1] = jnp.broadcast_to(ob_ref[...], (WIDTH, WIDTH)).T

    def forward(step):
        part = xr_buf.at[step, :, pl.ds(core * HALF, HALF)]
        return part, pltpu.make_async_remote_copy(
            src_ref=part, dst_ref=part, send_sem=f_send.at[step], recv_sem=f_recv.at[step],
            device_id=(sibling, col), device_id_type=MESH,
        )

    def arrive(step, carry):
        part, copy = forward(step)
        pltpu.make_async_copy(part, part, r_recv.at[step]).wait()
        copy.start()
        return carry

    lax.fori_loop(0, DEPTHS, arrive, 0)

    def arrive_too(step, carry):
        forward(step)[1].wait_recv()
        return carry

    lax.fori_loop(0, DEPTHS, arrive_too, 0)

    def straight(even, odd, lanes):
        even, odd = even.astype(F32), odd.astype(F32)
        top = jnp.where(lanes, even, odd).astype(BF16)
        bot = pltpu.roll(jnp.where(lanes, odd, even), TOK, 1).astype(BF16)
        return top, bot

    def align_right(z, carry):
        for k in range(4):
            even, odd = (
                xr_buf[z, e, 4 * k : 4 * k + 4].reshape(4 * LINES, WIDTH) for e in range(2)
            )
            top, bot = straight(even, odd, left_half)
            both = [v.reshape(4, LINES, WIDTH) for v in (top, bot)]
            r_buf[z, 4 * TOK * k : 4 * TOK * (k + 1), :] = jnp.concatenate(both, 1).reshape(
                4 * TOK, WIDTH
            )
        return carry

    lax.fori_loop(0, DEPTHS, align_right, 0)

    def plane_of(role, own, t):
        up = t if own else -1 - t
        return lax.rem(depth + (up if role == 1 else -up) + DEPTHS, DEPTHS)

    def hand(part, role):
        return pltpu.make_async_remote_copy(
            src_ref=given_buf.at[part, role], dst_ref=taken.at[part, 1 - role],
            send_sem=e_send.at[part, role], recv_sem=e_recv.at[part, 1 - role],
            device_id=(row, above if role == 0 else below), device_id_type=MESH,
        )

    def multiply(part, carry):
        rows = pl.ds(part * PART, PART)
        arrived = xl_buf.at[:, :, :, rows]
        pltpu.make_async_copy(arrived, arrived, l_recv.at[part]).wait()
        owns = []
        for role in range(2):
            own = []
            for z in range(role * REACH, (role + 1) * REACH):
                even, odd = (xl_buf[z, e, :, rows, :].reshape(HALF * PART, WIDTH) for e in range(2))
                both = [v.reshape(HALF, PART, WIDTH) for v in straight(even, odd, left_half)]
                own.append(jnp.concatenate(both, 1).reshape(HALF * 2 * PART, WIDTH))
            owns.append(jnp.concatenate(own, 1))
        for own_columns in (False, True):
            for role in range(2):
                for t in range(0, REACH, 2):
                    starts = [
                        pl.multiple_of(plane_of(role, own_columns, t + k) * 2 * TOK, 2 * TOK)
                        for k in range(2)
                    ]
                    others = jnp.concatenate(
                        [
                            jnp.concatenate(
                                [r_buf[z, pl.ds(start, 2 * TOK), :] for start in starts], 0
                            )
                            for z in range(role * REACH, (role + 1) * REACH)
                        ],
                        1,
                    )
                    v = lax.dot_general(owns[role], others, NT, preferred_element_type=F32)
                    for k in range(2):
                        w = v[:, k * WIDTH : (k + 1) * WIDTH]
                        if own_columns:
                            kept[part, role, t + k] = w
                        else:
                            given_buf[part, role, t + k] = w.astype(BF16)
                if not own_columns:
                    hand(part, role).start()
        return carry

    lax.fori_loop(0, PARTS, multiply, 0)

    def give(part, carry):
        for role in range(2):
            hand(part, 1 - role).wait_recv()
        for t in range(REACH - 1, -1, -1):
            for role in range(2):
                w = kept[part, role, t] + taken[part, role, t].astype(F32)
                for r in range(HALF):
                    top = w[2 * PART * r : 2 * PART * r + PART]
                    bot = w[2 * PART * r + PART : 2 * PART * (r + 1)]
                    even = jnp.where(left_half, top, pltpu.roll(bot, TOK, 1))
                    odd = jnp.where(left_half, pltpu.roll(top, TOK, 1), bot)
                    p_buf[part, role, t, 0, r] = even.astype(BF16)
                    p_buf[part, role, t, 1, r] = odd.astype(BF16)
                plane = plane_of(role, True, t)
                dst = q_ref.at[channels[role], pl.ds(part * PART, PART)]
                for u in range(HALF):
                    r = lax.rem(slot + u, HALF)
                    for e in range(2):
                        src = p_buf.at[part, role, t, sides[e], r]

                        def remote(src=src, dst=dst, r=r, plane=plane, e=e):
                            pltpu.make_async_remote_copy(
                                src_ref=src, dst_ref=dst,
                                send_sem=p_send.at[part], recv_sem=p_recv.at[part],
                                device_id=(core * HALF + r, plane * 2 + sides[e]),
                                device_id_type=MESH,
                            ).start()

                        def local(src=src, dst=dst):
                            pltpu.make_async_copy(src, dst, p_recv.at[part]).start()

                        if t == 0 and u == 0 and e == 0:
                            pl.when(itself)(local)
                            pl.when(apart)(remote)
                        else:
                            remote()
        return carry

    lax.fori_loop(0, PARTS, give, 0)

    def put(part):
        rows = pl.ds(part * PART, PART)
        return pltpu.make_async_copy(out_buf.at[:, rows], out_ref.at[:, rows], out_sem.at[part])

    def finish(part, carry):
        come = q_ref.at[:, pl.ds(part * PART, PART)]
        pltpu.make_async_copy(come, come, p_recv.at[part]).wait()
        turned = jnp.swapaxes(q_ref[:, pl.ds(part * PART, PART), :], 0, 1)
        for u in range(PART):
            v = turned[u].astype(F32)
            v = v - jnp.mean(v, axis=0, keepdims=True)
            spread = jnp.mean(v * v, axis=0, keepdims=True)
            n = (v * lax.rsqrt(spread + EPS) * wide_buf[0] + wide_buf[1]).astype(BF16)
            o = lax.dot_general(n, ow_ref[...], TN, preferred_element_type=F32)
            line = part * PART + u
            out_buf[0, line] = (gate_buf[line] * o[:TOK]).astype(BF16)
            out_buf[1, line] = (gate_buf[LINES + line] * o[TOK:]).astype(BF16)
        put(part).start()
        return carry

    lax.fori_loop(0, PARTS, finish, 0)

    def drain(step, carry):
        forward(step)[1].wait_send()
        return carry

    lax.fori_loop(0, DEPTHS, drain, 0)

    for part in range(PARTS):
        for role in range(2):
            hand(part, role).wait_send()

    def finished(n):
        for buf, sem in ((sr_buf, r_send), (sl_buf, l_send)):
            sent = buf.at[pl.ds(0, n)]
            pltpu.make_async_copy(sent, sent, sem).wait()
        for part in range(PARTS):
            given = q_ref.at[pl.ds(0, n), pl.ds(part * PART, PART)]
            pltpu.make_async_copy(given, given, p_send.at[part]).wait()

    pl.when(itself)(functools.partial(finished, WIDTH - 2))
    pl.when(apart)(functools.partial(finished, WIDTH))
    for part in range(PARTS):
        put(part).wait()


def exchange(mask, pair, wl, wr, wg, gain, bias, og, ob, ow):
    hbm = pl.BlockSpec(memory_space=pl.ANY)
    args = (mask, pair, wl, wr, wg, gain, bias, mask.reshape(DEPTHS, WIDTH), og, ob, ow)
    return pl.pallas_call(
        exchange_kernel,
        out_shape=jax.ShapeDtypeStruct((2, LINES, TOK, WIDTH), BF16),
        in_specs=[hbm] * len(args),
        out_specs=pl.BlockSpec(memory_space=pl.ANY),
        scratch_shapes=[
            pltpu.SMEM(mask.shape, mask.dtype),
            *(pltpu.VMEM(v.shape, v.dtype) for v in args[1:]),
            pltpu.SemaphoreType.DMA((len(args),)),
            pltpu.VMEM((TOK, TOK, WIDTH), BF16),
            pltpu.VMEM((PART, WIDTH, WIDTH), BF16),
            pltpu.VMEM((PART, WIDTH, WIDTH), BF16),
            pltpu.VMEM((WIDTH, LINES, WIDTH), BF16),
            pltpu.VMEM((WIDTH, LINES, WIDTH), BF16),
            pltpu.VMEM((2 * REACH, 2, ROWS, LINES, WIDTH), BF16),
            pltpu.VMEM((2 * REACH, 2, HALF, LINES, WIDTH), BF16),
            pltpu.VMEM((DEPTHS, ROWS * TOK, WIDTH), BF16),
            pltpu.VMEM((PARTS, 2, REACH, 2, HALF, PART, WIDTH), BF16),
            pltpu.VMEM((WIDTH, LINES, WIDTH), BF16),
            pltpu.VMEM((TOK, TOK, WIDTH), F32),
            pltpu.VMEM((2, WIDTH, WIDTH), F32),
            pltpu.VMEM((2, LINES, TOK, WIDTH), BF16),
            pltpu.VMEM((PARTS, 2, REACH, HALF * 2 * PART, WIDTH), F32),
            pltpu.VMEM((PARTS, 2, REACH, HALF * 2 * PART, WIDTH), BF16),
            pltpu.VMEM((PARTS, 2, REACH, HALF * 2 * PART, WIDTH), BF16),
            pltpu.SemaphoreType.DMA((PARTS,)),
            pltpu.SemaphoreType.DMA,
            pltpu.SemaphoreType.DMA,
            pltpu.SemaphoreType.DMA((DEPTHS,)),
            pltpu.SemaphoreType.DMA((PARTS,)),
            pltpu.SemaphoreType.DMA((DEPTHS,)),
            pltpu.SemaphoreType.DMA((DEPTHS,)),
            pltpu.SemaphoreType.DMA((PARTS,)),
            pltpu.SemaphoreType.DMA((PARTS,)),
            pltpu.SemaphoreType.DMA((PARTS, 2)),
            pltpu.SemaphoreType.DMA((PARTS, 2)),
        ],
        compiler_params=pltpu.CompilerParams(
            collective_id=0, has_side_effects=True, vmem_limit_bytes=LIMIT
        ),
        name="exchange",
    )(*args)


def shards(
    pair_rep,
    token_mask,
    in_gain,
    in_bias,
    left_weight,
    right_weight,
    gate_weight,
    out_gain,
    out_bias,
    out_weight,
):
    flat = lambda v: v.reshape(1, WIDTH)
    out = exchange(
        token_mask,
        pair_rep,
        left_weight,
        right_weight,
        gate_weight,
        flat(in_gain),
        flat(in_bias),
        flat(out_gain),
        flat(out_bias),
        out_weight,
    )
    return out.reshape(TOK, TOK, WIDTH)


def solution(mesh):
    placed = (P("row", "col", None), P(), P(), P(), P(), P(), P(), P(), P(), P())
    return jax.shard_map(
        shards, mesh=mesh, in_specs=placed, out_specs=P("row", "col", None), check_vma=False
    )
```

```python
import functools

import jax
import jax.numpy as jnp
from jax import lax
from jax.experimental import pallas as pl
from jax.experimental.pallas import tpu as pltpu
from jax.sharding import PartitionSpec as P

EPS = 1e-05
MESH = pl.DeviceIdType.MESH
F32 = jnp.float32
BF16 = jnp.bfloat16
NT = (((1,), (1,)), ((), ()))
TN = (((0,), (0,)), ((), ()))

ROWS = 16
COLS = 16
CHIPS = 8
DEPTHS = 8
TOK = 64
WIDTH = 128
LIMIT = 60 * 1024 * 1024
HALF = 8


def sigmoid(v):
    return 0.5 * jnp.tanh(0.5 * v) + 0.5


REACH = 4
PARTS = 2
LINES = TOK // 2
PART = LINES // PARTS


def exchange_kernel(
    mask_hbm, x_hbm, wl_hbm, wr_hbm, wg_hbm, gain_hbm, bias_hbm, valid_hbm,
    og_hbm, ob_hbm, ow_hbm,
    out_ref,
    mask_ref, x_ref, wl_ref, wr_ref, wg_ref, gain_ref, bias_ref, valid_ref,
    og_ref, ob_ref, ow_ref, in_sem,
    n_buf, tr_buf, tl_buf, sr_buf, sl_buf, xr_buf, xl_buf, r_buf, p_buf, q_ref, gate_buf, wide_buf, out_buf,
    kept, given_buf, taken,
    out_sem, r_send, l_send, r_recv, l_recv, f_send, f_recv, p_send, p_recv,
    e_send, e_recv,
):
    row, col = lax.axis_index("row"), lax.axis_index("col")
    core, half, chip, slot = lax.rem(row, 2), row // HALF, row // 2, lax.rem(row, HALF)
    depth, side = col // 2, lax.rem(col, 2)
    sibling = row + 1 - 2 * core
    above = lax.rem(depth + 1, DEPTHS) * 2 + side
    below = lax.rem(depth + DEPTHS - 1, DEPTHS) * 2 + side
    channels = (chip * COLS + col, chip * COLS + below)
    itself = half == core
    apart = jnp.logical_not(itself)

    loads = [
        pltpu.make_async_copy(src, dst, in_sem.at[k])
        for k, (src, dst) in enumerate(
            (
                (wl_hbm, wl_ref),
                (wr_hbm, wr_ref),
                (x_hbm, x_ref),
                (gain_hbm, gain_ref),
                (bias_hbm, bias_ref),
                (valid_hbm, valid_ref),
                (mask_hbm, mask_ref),
                (wg_hbm, wg_ref),
                (og_hbm, og_ref),
                (ob_hbm, ob_ref),
                (ow_hbm, ow_ref),
            )
        )
    ]
    for load in loads:
        load.start()

    barrier = pltpu.get_barrier_semaphore()

    def hello(to_row, to_col):
        pl.semaphore_signal(barrier, inc=1, device_id=(to_row, to_col), device_id_type=MESH)

    def greet(t, carry):
        to_col = lax.rem(col + t, COLS)
        for r in range(HALF):
            hello(core * HALF + r, to_col)
        return carry

    lax.fori_loop(1, COLS, greet, 0)
    for r in range(HALF):
        pl.when(core * HALF + r != row)(functools.partial(hello, core * HALF + r, col))

    @pl.when(apart)
    def _():
        hello(sibling, col)
        hello(row, above)
        hello(row, below)


    for load in loads:
        load.wait()

    gain, bias = gain_ref[...], bias_ref[...]
    wide = 2 * WIDTH
    eye = lax.broadcasted_iota(jnp.int32, (wide, wide), 0)
    eye = jnp.where(eye == lax.broadcasted_iota(jnp.int32, (wide, wide), 1), 1.0, 0.0).astype(BF16)
    weight = jnp.concatenate(
        [
            lax.dot_general(eye, w[...], NT, preferred_element_type=F32).astype(BF16)
            for w in (wl_ref, wr_ref)
        ],
        1,
    )
    blank = jnp.zeros((TOK, WIDTH), BF16)
    lane = lax.broadcasted_iota(jnp.int32, (1, WIDTH), 1)
    held = valid_ref[pl.ds(depth, 1), :].astype(F32)
    near = jnp.where(side == 0, 1, 0) == jnp.where(lane < TOK, 1, 0)
    held = jnp.where(near, held, pltpu.roll(held, TOK, 1))

    left_half = lane < TOK

    def project(part):
        def eight(w, carry):
            for u in range(8):
                line = part * PART + 8 * w + u
                first, second = line + LINES * side, line + LINES * (1 - side)
                v = jnp.concatenate([x_ref[first], x_ref[second]], 0).astype(F32)
                v = v - jnp.mean(v, axis=-1, keepdims=True)
                spread = jnp.mean(v * v, axis=-1, keepdims=True)
                n = (v * lax.rsqrt(spread + EPS) * gain + bias).astype(BF16)
                n_buf[first] = n[:TOK]
                n_buf[second] = n[TOK:]
                empty = jnp.concatenate([blank, blank], 0)
                both = jnp.concatenate(
                    [jnp.concatenate([empty, n], 0), jnp.concatenate([n, empty], 0)], 1
                )
                d = lax.dot_general(weight, both, NT, preferred_element_type=F32)
                e = sigmoid(d[:WIDTH]) * d[WIDTH:]
                one = mask_ref[row * TOK + first].astype(F32)
                two = mask_ref[row * TOK + second].astype(F32)
                m = held * jnp.where(left_half, one, two)
                tr_buf[8 * w + u] = (e[:, :WIDTH] * m).astype(BF16)
                tl_buf[8 * w + u] = (e[:, WIDTH:] * m).astype(BF16)
            return carry

        lax.fori_loop(0, PART // 8, eight, 0)
        rows = pl.ds(part * PART, PART)
        sr_buf[:, rows, :] = jnp.swapaxes(tr_buf[...], 0, 1)
        sl_buf[:, rows, :] = jnp.swapaxes(tl_buf[...], 0, 1)

    chips = [lax.rem(chip + d, CHIPS) for d in range(CHIPS)]
    sides = [side, 1 - side]

    def send(buf, dst_of, send_sem, sem_of, part):
        rows = pl.ds(part * PART, PART)

        def send_to(role, reach, d, e, alone):
            plane = lax.rem(depth + (reach if role == 0 else DEPTHS - reach), DEPTHS)
            owner = plane if role == 0 else lax.rem(plane + DEPTHS - 1, DEPTHS)
            src = buf.at[chips[d] * COLS + owner * 2 + sides[e], rows]
            step = role * REACH + reach
            dst = dst_of(step)

            def remote():
                pltpu.make_async_remote_copy(
                    src_ref=src, dst_ref=dst, send_sem=send_sem, recv_sem=sem_of(step),
                    device_id=(chips[d] * 2 + half, plane * 2 + sides[e]), device_id_type=MESH,
                ).start()

            def local():
                pltpu.make_async_copy(src, dst, sem_of(step)).start()

            if alone:
                pl.when(itself)(local)
                pl.when(apart)(remote)
            else:
                remote()

        def far(u, carry):
            for d in range(CHIPS):
                for e in range(2):
                    for role in range(2):
                        send_to(role, 1 + u, d, e, False)
            return carry

        lax.fori_loop(0, REACH - 1, far, 0)
        for d in range(CHIPS):
            for e in range(2):
                for role in range(2):
                    send_to(role, 0, d, e, d == 0 and e == 0)

    def send_right(part):
        rows = pl.ds(part * PART, PART)
        send(
            sr_buf, lambda step: xr_buf.at[step, side, row, rows],
            r_send, lambda step: r_recv.at[step], part,
        )

    def send_left(part, carry):
        rows = pl.ds(part * PART, PART)
        send(
            sl_buf, lambda step: xl_buf.at[step, side, slot, rows],
            l_send, lambda step: l_recv.at[part], part,
        )
        return carry

    project(0)

    @pl.when(itself)
    def _():
        pl.semaphore_wait(barrier, CHIPS * COLS)

    @pl.when(apart)
    def _():
        pl.semaphore_wait(barrier, CHIPS * COLS + 2)

    send_right(0)
    project(1)
    send_right(1)
    lax.fori_loop(0, PARTS, send_left, 0)

    def gates(u, carry):
        n = n_buf[pl.ds(4 * u, 4)].reshape(4 * TOK, WIDTH)
        gate = sigmoid(jnp.dot(n, wg_ref[...], preferred_element_type=F32))
        gate_buf[pl.ds(4 * u, 4)] = gate.reshape(4, TOK, WIDTH)
        return carry

    lax.fori_loop(0, TOK // 4, gates, 0)
    wide_buf[0] = jnp.broadcast_to(og_ref[...], (WIDTH, WIDTH)).T
    wide_buf[1] = jnp.broadcast_to(ob_ref[...], (WIDTH, WIDTH)).T

    def forward(step):
        part = xr_buf.at[step, :, pl.ds(core * HALF, HALF)]
        return part, pltpu.make_async_remote_copy(
            src_ref=part, dst_ref=part, send_sem=f_send.at[step], recv_sem=f_recv.at[step],
            device_id=(sibling, col), device_id_type=MESH,
        )

    def arrive(step, carry):
        part, copy = forward(step)
        pltpu.make_async_copy(part, part, r_recv.at[step]).wait()
        copy.start()
        return carry

    lax.fori_loop(0, DEPTHS, arrive, 0)

    def arrive_too(step, carry):
        forward(step)[1].wait_recv()
        return carry

    lax.fori_loop(0, DEPTHS, arrive_too, 0)

    def straight(even, odd, lanes):
        even, odd = even.astype(F32), odd.astype(F32)
        top = jnp.where(lanes, even, odd).astype(BF16)
        bot = pltpu.roll(jnp.where(lanes, odd, even), TOK, 1).astype(BF16)
        return top, bot

    def align_right(z, carry):
        for k in range(4):
            even, odd = (
                xr_buf[z, e, 4 * k : 4 * k + 4].reshape(4 * LINES, WIDTH) for e in range(2)
            )
            top, bot = straight(even, odd, left_half)
            both = [v.reshape(4, LINES, WIDTH) for v in (top, bot)]
            r_buf[z, 4 * TOK * k : 4 * TOK * (k + 1), :] = jnp.concatenate(both, 1).reshape(
                4 * TOK, WIDTH
            )
        return carry

    lax.fori_loop(0, DEPTHS, align_right, 0)

    def plane_of(role, own, t):
        up = t if own else -1 - t
        return lax.rem(depth + (up if role == 1 else -up) + DEPTHS, DEPTHS)

    def hand(part, role):
        return pltpu.make_async_remote_copy(
            src_ref=given_buf.at[part, role], dst_ref=taken.at[part, 1 - role],
            send_sem=e_send.at[part, role], recv_sem=e_recv.at[part, 1 - role],
            device_id=(row, above if role == 0 else below), device_id_type=MESH,
        )

    def multiply(part, carry):
        rows = pl.ds(part * PART, PART)
        arrived = xl_buf.at[:, :, :, rows]
        pltpu.make_async_copy(arrived, arrived, l_recv.at[part]).wait()
        owns = []
        for role in range(2):
            own = []
            for z in range(role * REACH, (role + 1) * REACH):
                even, odd = (xl_buf[z, e, :, rows, :].reshape(HALF * PART, WIDTH) for e in range(2))
                both = [v.reshape(HALF, PART, WIDTH) for v in straight(even, odd, left_half)]
                own.append(jnp.concatenate(both, 1).reshape(HALF * 2 * PART, WIDTH))
            owns.append(jnp.concatenate(own, 1))
        for own_columns in (False, True):
            for role in range(2):
                for t in range(0, REACH, 2):
                    starts = [
                        pl.multiple_of(plane_of(role, own_columns, t + k) * 2 * TOK, 2 * TOK)
                        for k in range(2)
                    ]
                    others = jnp.concatenate(
                        [
                            jnp.concatenate(
                                [r_buf[z, pl.ds(start, 2 * TOK), :] for start in starts], 0
                            )
                            for z in range(role * REACH, (role + 1) * REACH)
                        ],
                        1,
                    )
                    v = lax.dot_general(owns[role], others, NT, preferred_element_type=F32)
                    for k in range(2):
                        w = v[:, k * WIDTH : (k + 1) * WIDTH]
                        if own_columns:
                            kept[part, role, t + k] = w
                        else:
                            given_buf[part, role, t + k] = w.astype(BF16)
                if not own_columns:
                    hand(part, role).start()
        return carry

    lax.fori_loop(0, PARTS, multiply, 0)

    def give(part, carry):
        for role in range(2):
            hand(part, 1 - role).wait_recv()
        for t in range(REACH - 1, -1, -1):
            for role in range(2):
                w = kept[part, role, t] + taken[part, role, t].astype(F32)
                for r in range(HALF):
                    top = w[2 * PART * r : 2 * PART * r + PART]
                    bot = w[2 * PART * r + PART : 2 * PART * (r + 1)]
                    even = jnp.where(left_half, top, pltpu.roll(bot, TOK, 1))
                    odd = jnp.where(left_half, pltpu.roll(top, TOK, 1), bot)
                    p_buf[part, role, t, 0, r] = even.astype(BF16)
                    p_buf[part, role, t, 1, r] = odd.astype(BF16)
                plane = plane_of(role, True, t)
                dst = q_ref.at[channels[role], pl.ds(part * PART, PART)]
                for u in range(HALF):
                    r = lax.rem(slot + u, HALF)
                    for e in range(2):
                        src = p_buf.at[part, role, t, sides[e], r]

                        def remote(src=src, dst=dst, r=r, plane=plane, e=e):
                            pltpu.make_async_remote_copy(
                                src_ref=src, dst_ref=dst,
                                send_sem=p_send.at[part], recv_sem=p_recv.at[part],
                                device_id=(core * HALF + r, plane * 2 + sides[e]),
                                device_id_type=MESH,
                            ).start()

                        def local(src=src, dst=dst):
                            pltpu.make_async_copy(src, dst, p_recv.at[part]).start()

                        if t == 0 and u == 0 and e == 0:
                            pl.when(itself)(local)
                            pl.when(apart)(remote)
                        else:
                            remote()
        return carry

    lax.fori_loop(0, PARTS, give, 0)

    def put(part):
        rows = pl.ds(part * PART, PART)
        return pltpu.make_async_copy(out_buf.at[:, rows], out_ref.at[:, rows], out_sem.at[part])

    def finish(part, carry):
        come = q_ref.at[:, pl.ds(part * PART, PART)]
        pltpu.make_async_copy(come, come, p_recv.at[part]).wait()
        turned = jnp.swapaxes(q_ref[:, pl.ds(part * PART, PART), :], 0, 1)
        for u in range(PART):
            v = turned[u].astype(F32)
            v = v - jnp.mean(v, axis=0, keepdims=True)
            spread = jnp.mean(v * v, axis=0, keepdims=True)
            n = (v * lax.rsqrt(spread + EPS) * wide_buf[0] + wide_buf[1]).astype(BF16)
            o = lax.dot_general(n, ow_ref[...], TN, preferred_element_type=F32)
            line = part * PART + u
            out_buf[0, line] = (gate_buf[line] * o[:TOK]).astype(BF16)
            out_buf[1, line] = (gate_buf[LINES + line] * o[TOK:]).astype(BF16)
        put(part).start()
        return carry

    lax.fori_loop(0, PARTS, finish, 0)

    def drain(step, carry):
        forward(step)[1].wait_send()
        return carry

    lax.fori_loop(0, DEPTHS, drain, 0)

    for part in range(PARTS):
        for role in range(2):
            hand(part, role).wait_send()

    def finished(n):
        for buf, sem in ((sr_buf, r_send), (sl_buf, l_send)):
            sent = buf.at[pl.ds(0, n)]
            pltpu.make_async_copy(sent, sent, sem).wait()
        for part in range(PARTS):
            given = q_ref.at[pl.ds(0, n), pl.ds(part * PART, PART)]
            pltpu.make_async_copy(given, given, p_send.at[part]).wait()

    pl.when(itself)(functools.partial(finished, WIDTH - 2))
    pl.when(apart)(functools.partial(finished, WIDTH))
    for part in range(PARTS):
        put(part).wait()


def exchange(mask, pair, wl, wr, wg, gain, bias, og, ob, ow):
    hbm = pl.BlockSpec(memory_space=pl.ANY)
    args = (mask, pair, wl, wr, wg, gain, bias, mask.reshape(DEPTHS, WIDTH), og, ob, ow)
    return pl.pallas_call(
        exchange_kernel,
        out_shape=jax.ShapeDtypeStruct((2, LINES, TOK, WIDTH), BF16),
        in_specs=[hbm] * len(args),
        out_specs=pl.BlockSpec(memory_space=pl.ANY),
        scratch_shapes=[
            pltpu.SMEM(mask.shape, mask.dtype),
            *(pltpu.VMEM(v.shape, v.dtype) for v in args[1:]),
            pltpu.SemaphoreType.DMA((len(args),)),
            pltpu.VMEM((TOK, TOK, WIDTH), BF16),
            pltpu.VMEM((PART, WIDTH, WIDTH), BF16),
            pltpu.VMEM((PART, WIDTH, WIDTH), BF16),
            pltpu.VMEM((WIDTH, LINES, WIDTH), BF16),
            pltpu.VMEM((WIDTH, LINES, WIDTH), BF16),
            pltpu.VMEM((2 * REACH, 2, ROWS, LINES, WIDTH), BF16),
            pltpu.VMEM((2 * REACH, 2, HALF, LINES, WIDTH), BF16),
            pltpu.VMEM((DEPTHS, ROWS * TOK, WIDTH), BF16),
            pltpu.VMEM((PARTS, 2, REACH, 2, HALF, PART, WIDTH), BF16),
            pltpu.VMEM((WIDTH, LINES, WIDTH), BF16),
            pltpu.VMEM((TOK, TOK, WIDTH), F32),
            pltpu.VMEM((2, WIDTH, WIDTH), F32),
            pltpu.VMEM((2, LINES, TOK, WIDTH), BF16),
            pltpu.VMEM((PARTS, 2, REACH, HALF * 2 * PART, WIDTH), F32),
            pltpu.VMEM((PARTS, 2, REACH, HALF * 2 * PART, WIDTH), BF16),
            pltpu.VMEM((PARTS, 2, REACH, HALF * 2 * PART, WIDTH), BF16),
            pltpu.SemaphoreType.DMA((PARTS,)),
            pltpu.SemaphoreType.DMA,
            pltpu.SemaphoreType.DMA,
            pltpu.SemaphoreType.DMA((DEPTHS,)),
            pltpu.SemaphoreType.DMA((PARTS,)),
            pltpu.SemaphoreType.DMA((DEPTHS,)),
            pltpu.SemaphoreType.DMA((DEPTHS,)),
            pltpu.SemaphoreType.DMA((PARTS,)),
            pltpu.SemaphoreType.DMA((PARTS,)),
            pltpu.SemaphoreType.DMA((PARTS, 2)),
            pltpu.SemaphoreType.DMA((PARTS, 2)),
        ],
        compiler_params=pltpu.CompilerParams(
            collective_id=0, has_side_effects=True, vmem_limit_bytes=LIMIT
        ),
        name="exchange",
    )(*args)


def shards(
    pair_rep,
    token_mask,
    in_gain,
    in_bias,
    left_weight,
    right_weight,
    gate_weight,
    out_gain,
    out_bias,
    out_weight,
):
    flat = lambda v: v.reshape(1, WIDTH)
    out = exchange(
        token_mask,
        pair_rep,
        left_weight,
        right_weight,
        gate_weight,
        flat(in_gain),
        flat(in_bias),
        flat(out_gain),
        flat(out_bias),
        out_weight,
    )
    return out.reshape(TOK, TOK, WIDTH)


def solution(mesh):
    placed = (P("row", "col", None), P(), P(), P(), P(), P(), P(), P(), P(), P())
    return jax.shard_map(
        shards, mesh=mesh, in_specs=placed, out_specs=P("row", "col", None), check_vma=False
    )
```
